128 devices in a mesh: rec: 4 (over y), ctx: 32 (over x, z, core).
Axes of the slice: x: 4, y: 4, z: 4, core: 2. Of those that a mesh axis runs over, the one named last changes fastest.
Arguments:
- queries: bfloat16 [4, 1024, 2048], P('rec', 'ctx'), may hold values from -360 to 360
- grad_out: bfloat16 [4, 1024, 2048], P('rec', 'ctx'), may hold values from -6 to 6
- keys: bfloat16 [4096, 2048], P('ctx'), may hold values from -13 to 13
- values: bfloat16 [4096, 2048], P('ctx'), may hold values from -6 to 6
- surv_index: int32 [4, 1024], P('rec'), may hold values from 0 to 127, as said below
- counts: int32 [4, 32], P('rec'), may hold values from 1 to 32, as said below
Outputs:
- query_grad: bfloat16 [4, 1024, 2048], P('rec', 'ctx')
- key_grad: bfloat16 [4096, 2048], P('ctx', 'rec')
- value_grad: bfloat16 [4096, 2048], P('ctx', 'rec')
The draws below stay inside these ranges and needn't reach their ends.
Inputs may be any that keep to these rules, and one draw needn't show every extreme that they name: `surv_index`: in each depth and index of ctx the live slots come first and hold distinct positions in increasing order; the other slots hold 0. In each depth and index of ctx whose 32 slots are all live, one live slot holds position 127. `counts`: in every depth some index of ctx has all 32 slots live.
All inputs are finite; a program needn't handle non-finite values.
Results may differ from the reference program's by a relative error of at most 0.0051.
Values may be sent and summed in bfloat16 or wider, within the bound.
No kernel may reach another device: no remote copies, remote signals or barrier semaphores. Data moves between devices by JAX's collectives and lax.ppermute only.
A program may use at most 64 MiB of HBM per device.

```python
import math
import jax
import jax.numpy as jnp
from jax import lax

HEADS = 16
HEAD_DIM = 128
TOK_DEV = 128
CAP = 32
DEPTHS = 4
TOKENS = 4096
CAPS = 1024
HD = 2048
N_CTX = 32


def key_rows(random_seed_key):
    normals = jax.random.normal(jax.random.fold_in(random_seed_key, 11), (TOKENS, HEADS * HEAD_DIM), jnp.float32)
    normals = jnp.clip(normals, -6.0, 6.0)
    return normals


def draw_keys(key, part):
    return key_rows(key).astype(jnp.bfloat16)


def draw_queries(key, part):
    slot_total = CAP * N_CTX
    normals = jax.random.normal(jax.random.fold_in(key, 21), (DEPTHS, slot_total, HEADS * HEAD_DIM), jnp.float32)
    normals = jnp.clip(normals, -6.0, 6.0)
    return normals.astype(jnp.bfloat16)


def remaining_token_counts(random_seed_key):
    drawn = jax.random.randint(jax.random.fold_in(random_seed_key, 31), (DEPTHS, N_CTX), 1, CAP + 1)
    fullest = jax.random.randint(jax.random.fold_in(random_seed_key, 32), (DEPTHS, 1), 0, N_CTX)
    return jnp.where(jnp.arange(N_CTX)[None, :] == fullest, CAP, drawn).astype(jnp.int32)


def draw_counts(key, part):
    return remaining_token_counts(key)


def draw_surv_index(key, part):
    active_count_list = remaining_token_counts(key)
    rank_keys = jax.random.randint(jax.random.fold_in(key, 33), (DEPTHS, N_CTX, TOK_DEV), 0, 2 ** 18)
    rank_keys = rank_keys * TOK_DEV + jnp.arange(TOK_DEV)[None, None, :]
    lastpos = jnp.arange(TOK_DEV) == TOK_DEV - 1
    rank_keys = jnp.where(lastpos[None, None, :] & (active_count_list[:, :, None] == CAP), -1, rank_keys)
    ordering = jnp.argsort(rank_keys, axis=-1).astype(jnp.int32)
    chosen = ordering[:, :, :CAP]
    is_live = jnp.arange(CAP)[None, None, :] < active_count_list[:, :, None]
    marked = jnp.where(is_live, chosen, TOK_DEV)
    ordered = jnp.sort(marked, axis=-1)
    indices = jnp.where(ordered == TOK_DEV, 0, ordered)
    return indices.reshape(DEPTHS, N_CTX * CAP).astype(jnp.int32)


def block_levels(key, shape, shards, smallest, top_value):
    gain, own = 1.0, jax.random.fold_in(key, 6)
    for position, shards_of in shards:
        heights = jnp.exp(jax.random.uniform(jax.random.fold_in(own, position), (shards_of,), jnp.float32, smallest / len(shards), top_value / len(shards)))
        gain = gain * jnp.repeat(heights, shape[position] // shards_of).reshape([-1 if axis == position else 1 for axis in range(len(shape))])
    return gain


def bell_draw(key, extent, scale, reach, pieces=(), kind=jnp.bfloat16):
    array = jax.random.normal(key, extent, jnp.float32) * scale
    if len(pieces) > 0:
        array = block_levels(key, extent, pieces, -0.22, 0.18) * array
    return jnp.clip(array, min=-reach, max=reach).astype(kind)


def setup_inputs(seed: int = 0) -> dict:
    streams_of = jax.random.split(jax.random.key(seed), 7)
    return {
        "queries": draw_queries(jax.random.fold_in(streams_of[6], 71), 0),
        "grad_out": bell_draw(streams_of[1], (DEPTHS, CAPS, HD), 1.0, 6.0, ((0, 4), (1, 32))),
        "keys": draw_keys(jax.random.fold_in(streams_of[6], 71), 0),
        "values": bell_draw(streams_of[3], (TOKENS, HD), 1.0, 6.0, ((0, 32),)),
        "surv_index": draw_surv_index(jax.random.fold_in(streams_of[6], 71), 0),
        "counts": draw_counts(jax.random.fold_in(streams_of[6], 71), 0),
    }


def rounded(array_in):
    return lax.optimization_barrier(array_in.astype(jnp.bfloat16)).astype(jnp.float32)

def depth_backward(depth_queries, depth_grads, surv_row, count_row, keys_split, value_pieces):
    slot_ids = jnp.arange(CAP * N_CTX)
    key_pos = jnp.arange(TOKENS)
    query_pos = slot_ids // CAP * TOK_DEV + surv_row
    is_live = slot_ids % CAP < jnp.repeat(count_row, CAP)
    visible = key_pos[None, :] <= query_pos[:, None]
    factor = 1.0 / math.sqrt(HEAD_DIM)
    query_split = depth_queries.astype(jnp.float32).reshape(CAP * N_CTX, HEADS, HEAD_DIM).transpose(1, 0, 2)
    masked_grads = jnp.where(is_live[:, None], depth_grads.astype(jnp.float32), 0.0)
    grad_split = masked_grads.reshape(CAP * N_CTX, HEADS, HEAD_DIM).transpose(1, 0, 2)

    def per_head(operands):
        query_head, grad_head, key_head, value_head = operands
        score_matrix = factor * jnp.dot(query_head, key_head.T, precision=lax.Precision.HIGHEST)
        row_max = lax.optimization_barrier(jnp.max(jnp.where(visible, score_matrix, -jnp.inf), axis=1))
        row_sum = lax.optimization_barrier(jnp.sum(jnp.where(visible, jnp.exp(score_matrix - row_max[:, None]), 0.0), axis=1))
        log_total = row_max + jnp.log(row_sum)
        weights = jnp.where(visible, jnp.exp(score_matrix - log_total[:, None]), 0.0)
        grad_weights = jnp.dot(grad_head, value_head.T, precision=lax.Precision.HIGHEST)
        row_delta = lax.optimization_barrier(jnp.sum(weights * grad_weights, axis=1))
        grad_scores = rounded(weights * (grad_weights - row_delta[:, None]))
        low_weights = rounded(weights)
        query_term = factor * jnp.dot(grad_scores, key_head, precision=lax.Precision.HIGHEST)
        key_term = factor * jnp.dot(grad_scores.T, query_head, precision=lax.Precision.HIGHEST)
        value_term = jnp.dot(low_weights.T, grad_head, precision=lax.Precision.HIGHEST)
        return (query_term, key_term, value_term)
    return lax.map(per_head, (query_split, grad_split, keys_split, value_pieces))

def reference(queries, grad_out, keys, values, surv_index, counts):
    keys_split = keys.astype(jnp.float32).reshape(TOKENS, HEADS, HEAD_DIM).transpose(1, 0, 2)
    value_pieces = values.astype(jnp.float32).reshape(TOKENS, HEADS, HEAD_DIM).transpose(1, 0, 2)

    def per_depth(totals, operands):
        depth_queries, depth_grads, surv_row, count_row = operands
        query_term, key_term, value_term = depth_backward(depth_queries, depth_grads, surv_row, count_row, keys_split, value_pieces)
        return ((totals[0] + key_term, totals[1] + value_term), query_term)
    empty_sum = jnp.zeros((HEADS, TOKENS, HEAD_DIM), jnp.float32)
    sums, query_terms = lax.scan(per_depth, (empty_sum, empty_sum), (queries, grad_out, surv_index, counts))
    query_grad = query_terms.transpose(0, 2, 1, 3).reshape(DEPTHS, CAP * N_CTX, HEADS * HEAD_DIM).astype(jnp.bfloat16)
    key_grad = sums[0].transpose(1, 0, 2).reshape(TOKENS, HEADS * HEAD_DIM).astype(jnp.bfloat16)
    value_grad = sums[1].transpose(1, 0, 2).reshape(TOKENS, HEADS * HEAD_DIM).astype(jnp.bfloat16)
    return (query_grad, key_grad, value_grad)
```

```python
import math

import jax
import jax.numpy as jnp
from jax import lax
from jax.experimental import pallas as pl
from jax.experimental.pallas import tpu as pltpu
from jax.sharding import Mesh
from jax.sharding import PartitionSpec as P

HEADS = 16
HEAD_DIM = 128
CAP = 32
TOK = 128
X, Z, C = "ctx_0", "ctx_1", "ctx_2"
CTX = (X, Z, C)
GROUPS = 4
CHUNK = 512
QG_ROWS = 72
FACTOR = 1.0 / math.sqrt(HEAD_DIM)
LOG2E = 1.4426950408889634
NEG_FILL = -1e30

NT = (((1,), (1,)), ((), ()))
TN = (((0,), (0,)), ((), ()))
NN = (((1,), (0,)), ((), ()))


def dot(a, b, dims):
    return lax.dot_general(a, b, dims, preferred_element_type=jnp.float32)


def folded(a, op):
    return op(a.reshape(-1, 8, a.shape[1]), axis=0)


def attention_kernel(qg, own, oth, dq, d_own, d_oth, s_buf, w_buf, a_own, a_oth):
    core = lax.axis_index(C)
    place = 2 * lax.axis_index(Z) + core
    sides = ((own, a_own, core), (oth, a_oth, 1 - core))
    rows = lax.broadcasted_iota(jnp.int32, (CHUNK, TOK), 0)
    spread = rows + rows // TOK * TOK
    for x in reversed(range(GROUPS)):
        q = jnp.concatenate([qg[4 * y + x, 0:CAP, :] for y in range(4)], axis=0)
        g = jnp.concatenate([qg[4 * y + x, CAP : 2 * CAP, :] for y in range(4)], axis=0)
        where = sum(qg[4 * y + x, 2 * CAP : 2 * CAP + 8, :].astype(jnp.float32) for y in range(4))
        slot_pos = where[0:1, :].astype(jnp.int32) + (8 * x + place) * TOK
        chunks = [(s, k) for k in range(x + 1) for s in range(2)]
        top = jnp.full((8, TOK), NEG_FILL, jnp.float32)
        for s, k in chunks:
            ref, _, part = sides[s]
            at = slice(k * CHUNK, (k + 1) * CHUNK)
            score = dot(ref[at, 0:HEAD_DIM], q, NT)
            if k == x:
                key_pos = spread + (2 * k * CHUNK + part * TOK)
                score = jnp.where(key_pos <= slot_pos, score, NEG_FILL)
            s_buf[s, at, :] = score
            top = jnp.maximum(top, folded(score, jnp.max))
        top = jnp.max(top, axis=0, keepdims=True)
        total = jnp.zeros((8, TOK), jnp.float32)
        weighted = jnp.zeros((8, TOK), jnp.float32)
        for s, k in chunks:
            ref = sides[s][0]
            at = slice(k * CHUNK, (k + 1) * CHUNK)
            e = jnp.exp2((s_buf[s, at, :] - top) * (FACTOR * LOG2E))
            dw = dot(ref[at, HEAD_DIM : 2 * HEAD_DIM], g, NT)
            s_buf[s, at, :] = e
            w_buf[s, at, :] = dw
            total = total + folded(e, jnp.sum)
            weighted = weighted + folded(e * dw, jnp.sum)
        scale = 1.0 / jnp.sum(total, axis=0, keepdims=True)
        delta = jnp.sum(weighted, axis=0, keepdims=True) * scale
        query_sum = jnp.zeros((TOK, HEAD_DIM), jnp.float32)
        for s, k in chunks:
            ref, acc, _ = sides[s]
            at = slice(k * CHUNK, (k + 1) * CHUNK)
            w = s_buf[s, at, :] * scale
            ds = (w * (w_buf[s, at, :] - delta)).astype(jnp.bfloat16)
            wb = w.astype(jnp.bfloat16)
            query_sum = query_sum + dot(ds, ref[at, 0:HEAD_DIM], TN)
            key_part = dot(ds, q, NN)
            value_part = dot(wb, g, NN)
            if x == GROUPS - 1:
                acc[at, 0:HEAD_DIM] = key_part
                acc[at, HEAD_DIM : 2 * HEAD_DIM] = value_part
            else:
                acc[at, 0:HEAD_DIM] += key_part
                acc[at, HEAD_DIM : 2 * HEAD_DIM] += value_part
        query_out = (query_sum * FACTOR).astype(jnp.bfloat16)
        for y in range(4):
            dq[4 * y + x, :, :] = query_out[CAP * y : CAP * (y + 1), :]
    d_own[:, 0:HEAD_DIM] = a_own[:, 0:HEAD_DIM] * FACTOR
    d_own[:, HEAD_DIM:] = a_own[:, HEAD_DIM:]
    d_oth[:, 0:HEAD_DIM] = (a_oth[:, 0:HEAD_DIM] * FACTOR).astype(jnp.bfloat16)
    d_oth[:, HEAD_DIM:] = a_oth[:, HEAD_DIM:].astype(jnp.bfloat16)


def attention(qg, own, oth):
    keys = own.shape[0]
    vmem = pl.BlockSpec(memory_space=pltpu.VMEM)
    return pl.pallas_call(
        attention_kernel,
        out_shape=(
            jax.ShapeDtypeStruct((16, CAP, HEAD_DIM), jnp.bfloat16),
            jax.ShapeDtypeStruct((keys, 2 * HEAD_DIM), jnp.float32),
            jax.ShapeDtypeStruct((keys, 2 * HEAD_DIM), jnp.bfloat16),
        ),
        in_specs=[vmem] * 3,
        out_specs=(vmem,) * 3,
        scratch_shapes=[
            pltpu.VMEM((2, keys, TOK), jnp.float32),
            pltpu.VMEM((2, keys, TOK), jnp.float32),
            pltpu.VMEM((keys, 2 * HEAD_DIM), jnp.float32),
            pltpu.VMEM((keys, 2 * HEAD_DIM), jnp.float32),
        ],
        compiler_params=pltpu.CompilerParams(vmem_limit_bytes=40 * 2**20),
        cost_estimate=pl.CostEstimate(
            flops=2 * 10 * 128 * 1024 * 128 * 5, bytes_accessed=6 * 2**20, transcendentals=10 * 128 * 1024
        ),
    )(qg, own, oth)


def swap_cores(a):
    return lax.ppermute(a, C, [(0, 1), (1, 0)])


def body(queries, grad_out, keys, values, surv_index, counts):
    depth, ctx = lax.axis_index("rec"), lax.axis_index(CTX)
    def own_heads(a):
        cols = lax.dynamic_slice_in_dim(a, depth * 4 * HEAD_DIM, 4 * HEAD_DIM, axis=1)
        return cols.reshape(TOK, 4, HEAD_DIM).transpose(1, 0, 2)

    kv = jnp.concatenate((own_heads(keys), own_heads(values)), axis=2)
    kv = jnp.broadcast_to(kv[:, None], (4, 4, TOK, 2 * HEAD_DIM)).reshape(16, TOK, 2 * HEAD_DIM)
    kv = lax.all_to_all(kv, (X, Z), 0, 0, tiled=True).reshape(16 * TOK, 2 * HEAD_DIM)
    kv_other = swap_cores(kv)
    live = jnp.arange(CAP) < lax.dynamic_index_in_dim(counts[0], ctx, keepdims=False)
    own_grad = jnp.where(live[:, None], grad_out[0], jnp.zeros_like(grad_out[0]))
    where = lax.dynamic_slice_in_dim(surv_index[0], ctx * CAP, CAP)
    where = jnp.where(jnp.arange(TOK) // CAP == depth, jnp.tile(where, 4), 0).astype(jnp.bfloat16)

    def by_head(a):
        return a.reshape(CAP, HEADS, HEAD_DIM).transpose(1, 0, 2)

    qg = jnp.concatenate(
        (by_head(queries[0]), by_head(own_grad), jnp.broadcast_to(where[None, None], (16, QG_ROWS - 2 * CAP, TOK))),
        axis=1,
    )
    qg = lax.all_to_all(qg, ("rec", X), 0, 0, tiled=True)
    dq, d_own, d_other = attention(qg, kv, kv_other)
    dq = lax.all_to_all(dq, ("rec", X), 0, 0, tiled=True)
    query_grad = dq.transpose(1, 0, 2).reshape(1, CAP, HEADS * HEAD_DIM)
    mine = swap_cores(d_other)
    sums = (d_own + mine.astype(jnp.float32)).astype(jnp.bfloat16)
    sums = lax.all_to_all(sums.reshape(16, TOK, 2 * HEAD_DIM), (X, Z), 0, 0, tiled=True)
    sums = jnp.sum(sums.reshape(4, 4, TOK, 2 * HEAD_DIM).astype(jnp.float32), axis=1).astype(jnp.bfloat16)
    key_grad = sums[:, :, :HEAD_DIM].transpose(1, 0, 2).reshape(TOK, 4 * HEAD_DIM)
    value_grad = sums[:, :, HEAD_DIM:].transpose(1, 0, 2).reshape(TOK, 4 * HEAD_DIM)
    return query_grad, key_grad, value_grad


def solution(mesh):
    split = Mesh(mesh.devices.reshape(mesh.shape["rec"], 4, 4, 2), ("rec", X, Z, C))
    return jax.shard_map(
        body,
        mesh=split,
        in_specs=(
            P("rec", CTX, None),
            P("rec", CTX, None),
            P(CTX, None),
            P(CTX, None),
            P("rec", None),
            P("rec", None),
        ),
        out_specs=(P("rec", CTX, None), P(CTX, "rec"), P(CTX, "rec")),
        check_vma=False,
    )
```

```python
import math

import jax
import jax.numpy as jnp
from jax import lax
from jax.experimental import pallas as pl
from jax.experimental.pallas import tpu as pltpu
from jax.sharding import Mesh
from jax.sharding import PartitionSpec as P

HEADS = 16
HEAD_DIM = 128
CAP = 32
TOK = 128
X, Z, C = "ctx_0", "ctx_1", "ctx_2"
CTX = (X, Z, C)
GROUPS = 4
CHUNK = 512
QG_ROWS = 72
FACTOR = 1.0 / math.sqrt(HEAD_DIM)
LOG2E = 1.4426950408889634
NEG_FILL = -1e30

NT = (((1,), (1,)), ((), ()))
TN = (((0,), (0,)), ((), ()))
NN = (((1,), (0,)), ((), ()))


def dot(a, b, dims):
    return lax.dot_general(a, b, dims, preferred_element_type=jnp.float32)


def folded(a, op):
    return op(a.reshape(-1, 8, a.shape[1]), axis=0)


def attention_kernel(*refs):
    q_in, (own, oth) = refs[0:4], refs[4:6]
    q_out, (d_own, d_oth) = refs[6:10], refs[10:12]
    qg, dq, s_buf, w_buf, a_own, a_oth = refs[12:]
    core = lax.axis_index(C)
    here = lax.axis_index(X)
    place = 2 * lax.axis_index(Z) + core
    sides = ((own, a_own, core), (oth, a_oth, 1 - core))
    for p in range(4):
        qg[p] = q_in[p][...]
    rows = lax.broadcasted_iota(jnp.int32, (CHUNK, TOK), 0)
    spread = rows + rows // TOK * TOK
    for x in reversed(range(GROUPS)):
        from_x = lax.rem(here - x + 4, 4)
        q = jnp.concatenate([qg[from_x, o, 0:CAP, :] for o in range(4)], axis=0)
        g = jnp.concatenate([qg[from_x, o, CAP : 2 * CAP, :] for o in range(4)], axis=0)
        where = sum(qg[from_x, o, 2 * CAP : 2 * CAP + 8, :].astype(jnp.float32) for o in range(4))
        slot_pos = where[0:1, :].astype(jnp.int32) + (8 * x + place) * TOK
        chunks = [(s, k) for k in range(x + 1) for s in range(2)]
        top = jnp.full((8, TOK), NEG_FILL, jnp.float32)
        for s, k in chunks:
            ref, _, part = sides[s]
            at = slice(k * CHUNK, (k + 1) * CHUNK)
            score = dot(ref[at, 0:HEAD_DIM], q, NT)
            if k == x:
                key_pos = spread + (2 * k * CHUNK + part * TOK)
                score = jnp.where(key_pos <= slot_pos, score, NEG_FILL)
            s_buf[s, at, :] = score
            top = jnp.maximum(top, folded(score, jnp.max))
        top = jnp.max(top, axis=0, keepdims=True)
        total = jnp.zeros((8, TOK), jnp.float32)
        weighted = jnp.zeros((8, TOK), jnp.float32)
        for s, k in chunks:
            ref = sides[s][0]
            at = slice(k * CHUNK, (k + 1) * CHUNK)
            e = jnp.exp2((s_buf[s, at, :] - top) * (FACTOR * LOG2E))
            dw = dot(ref[at, HEAD_DIM : 2 * HEAD_DIM], g, NT)
            s_buf[s, at, :] = e
            w_buf[s, at, :] = dw
            total = total + folded(e, jnp.sum)
            weighted = weighted + folded(e * dw, jnp.sum)
        scale = 1.0 / jnp.sum(total, axis=0, keepdims=True)
        delta = jnp.sum(weighted, axis=0, keepdims=True) * scale
        query_sum = jnp.zeros((TOK, HEAD_DIM), jnp.float32)
        for s, k in chunks:
            ref, acc, _ = sides[s]
            at = slice(k * CHUNK, (k + 1) * CHUNK)
            w = s_buf[s, at, :] * scale
            ds = (w * (w_buf[s, at, :] - delta)).astype(jnp.bfloat16)
            wb = w.astype(jnp.bfloat16)
            query_sum = query_sum + dot(ds, ref[at, 0:HEAD_DIM], TN)
            key_part = dot(ds, q, NN)
            value_part = dot(wb, g, NN)
            if x == GROUPS - 1:
                acc[at, 0:HEAD_DIM] = key_part
                acc[at, HEAD_DIM : 2 * HEAD_DIM] = value_part
            else:
                acc[at, 0:HEAD_DIM] += key_part
                acc[at, HEAD_DIM : 2 * HEAD_DIM] += value_part
        dq[from_x] = (query_sum * FACTOR).astype(jnp.bfloat16).reshape(4, CAP, HEAD_DIM)
    for p in range(4):
        q_out[p][...] = dq[p]
    d_own[:, 0:HEAD_DIM] = a_own[:, 0:HEAD_DIM] * FACTOR
    d_own[:, HEAD_DIM:] = a_own[:, HEAD_DIM:]
    d_oth[:, 0:HEAD_DIM] = (a_oth[:, 0:HEAD_DIM] * FACTOR).astype(jnp.bfloat16)
    d_oth[:, HEAD_DIM:] = a_oth[:, HEAD_DIM:].astype(jnp.bfloat16)


def attention(qg, own, oth):
    keys = own.shape[0]
    vmem = pl.BlockSpec(memory_space=pltpu.VMEM)
    out = pl.pallas_call(
        attention_kernel,
        out_shape=(jax.ShapeDtypeStruct((4, CAP, HEAD_DIM), jnp.bfloat16),) * 4
        + (
            jax.ShapeDtypeStruct((keys, 2 * HEAD_DIM), jnp.float32),
            jax.ShapeDtypeStruct((keys, 2 * HEAD_DIM), jnp.bfloat16),
        ),
        in_specs=[vmem] * 6,
        out_specs=(vmem,) * 6,
        scratch_shapes=[
            pltpu.VMEM((4, 4, QG_ROWS, HEAD_DIM), jnp.bfloat16),
            pltpu.VMEM((4, 4, CAP, HEAD_DIM), jnp.bfloat16),
            pltpu.VMEM((2, keys, TOK), jnp.float32),
            pltpu.VMEM((2, keys, TOK), jnp.float32),
            pltpu.VMEM((keys, 2 * HEAD_DIM), jnp.float32),
            pltpu.VMEM((keys, 2 * HEAD_DIM), jnp.float32),
        ],
        compiler_params=pltpu.CompilerParams(vmem_limit_bytes=40 * 2**20),
        cost_estimate=pl.CostEstimate(
            flops=2 * 10 * 128 * 1024 * 128 * 5, bytes_accessed=6 * 2**20, transcendentals=10 * 128 * 1024
        ),
    )(*qg, own, oth)
    return out[0:4], out[4], out[5]


def pack_kernel(keys, values, queries, grad_out, surv_index, counts, kv, *rest):
    qg, (k_buf, v_buf, q_buf, g_buf, s_buf, c_buf, sems) = rest[0:4], rest[4:]
    depth = lax.axis_index("rec")
    ctx = lax.axis_index(X) * 8 + lax.axis_index(Z) * 2 + lax.axis_index(C)
    mine = pl.ds(pl.multiple_of(depth * 4 * HEAD_DIM, 4 * HEAD_DIM), 4 * HEAD_DIM)
    copies = [
        pltpu.make_async_copy(src, dst, sems.at[n])
        for n, (src, dst) in enumerate(
            (
                (keys.at[:, mine], k_buf),
                (values.at[:, mine], v_buf),
                (queries.at[0], q_buf),
                (grad_out.at[0], g_buf),
                (surv_index, s_buf),
                (counts, c_buf),
            )
        )
    ]
    for copy in copies:
        copy.start()
    copies[0].wait()
    copies[1].wait()
    for x in range(4):
        cols = slice(x * HEAD_DIM, (x + 1) * HEAD_DIM)
        for z in range(4):
            kv[4 * x + z, :, 0:HEAD_DIM] = k_buf[:, cols]
            kv[4 * x + z, :, HEAD_DIM:] = v_buf[:, cols]
    for copy in copies[2:]:
        copy.wait()
    live = lax.broadcasted_iota(jnp.int32, (CAP, HEAD_DIM), 0) < c_buf[0, ctx]
    quarter = lax.rem(ctx, 4)
    near = s_buf[0:1, pl.ds(pl.multiple_of(ctx // 4 * TOK, TOK), TOK)]
    lane_group = lax.broadcasted_iota(jnp.int32, (8, TOK), 1) // CAP
    for o in range(4):
        where = pltpu.roll(jnp.broadcast_to(near, (8, TOK)), lax.rem(o - quarter + 4, 4) * CAP, 1)
        where = jnp.where(lane_group == o, where, 0).astype(jnp.float32).astype(jnp.bfloat16)
        for x in range(4):
            head = lax.rem(depth + o, 4) * 4 + x
            cols = pl.ds(pl.multiple_of(head * HEAD_DIM, HEAD_DIM), HEAD_DIM)
            qg[o][x, 0:CAP, :] = q_buf[:, cols]
            grad = jnp.where(live, g_buf[:, cols].astype(jnp.float32), 0.0)
            qg[o][x, CAP : 2 * CAP, :] = grad.astype(jnp.bfloat16)
            qg[o][x, 2 * CAP :, :] = where


def pack(keys, values, queries, grad_out, surv_index, counts):
    vmem = pl.BlockSpec(memory_space=pltpu.VMEM)
    hbm = pl.BlockSpec(memory_space=pltpu.HBM)
    out = pl.pallas_call(
        pack_kernel,
        out_shape=(jax.ShapeDtypeStruct((16, TOK, 2 * HEAD_DIM), jnp.bfloat16),)
        + (jax.ShapeDtypeStruct((4, QG_ROWS, HEAD_DIM), jnp.bfloat16),) * 4,
        in_specs=[hbm] * 6,
        out_specs=(vmem,) * 5,
        scratch_shapes=[
            pltpu.VMEM((TOK, 4 * HEAD_DIM), jnp.bfloat16),
            pltpu.VMEM((TOK, 4 * HEAD_DIM), jnp.bfloat16),
            pltpu.VMEM((CAP, HEADS * HEAD_DIM), jnp.bfloat16),
            pltpu.VMEM((CAP, HEADS * HEAD_DIM), jnp.bfloat16),
            pltpu.VMEM(surv_index.shape, jnp.int32),
            pltpu.SMEM(counts.shape, jnp.int32),
            pltpu.SemaphoreType.DMA((6,)),
        ],
        compiler_params=pltpu.CompilerParams(vmem_limit_bytes=8 * 2**20),
    )(*(pltpu.with_memory_space_constraint(a, pltpu.HBM) for a in (keys, values, queries, grad_out, surv_index, counts)))
    return out[0], out[1:]


def unpack_kernel(parts, key_grad, value_grad, k_buf, v_buf, sems):
    sides = ((k_buf, key_grad, 0), (v_buf, value_grad, HEAD_DIM))
    copies = []
    for n, (buf, out, at) in enumerate(sides):
        for x in range(4):
            total = sum(parts[4 * x + z, :, at : at + HEAD_DIM].astype(jnp.float32) for z in range(4))
            buf[:, x * HEAD_DIM : (x + 1) * HEAD_DIM] = total.astype(jnp.bfloat16)
        copies.append(pltpu.make_async_copy(buf, out, sems.at[n]))
        copies[n].start()
    for copy in copies:
        copy.wait()


def unpack(parts):
    out = jax.ShapeDtypeStruct((TOK, 4 * HEAD_DIM), jnp.bfloat16)
    return pl.pallas_call(
        unpack_kernel,
        out_shape=(out, out),
        in_specs=[pl.BlockSpec(memory_space=pltpu.VMEM)],
        out_specs=(pl.BlockSpec(memory_space=pl.ANY),) * 2,
        scratch_shapes=[
            pltpu.VMEM((TOK, 4 * HEAD_DIM), jnp.bfloat16),
            pltpu.VMEM((TOK, 4 * HEAD_DIM), jnp.bfloat16),
            pltpu.SemaphoreType.DMA((2,)),
        ],
        compiler_params=pltpu.CompilerParams(vmem_limit_bytes=8 * 2**20),
    )(parts)


def moved(a, axis, by):
    return a if by % 4 == 0 else lax.ppermute(a, axis, [(i, (i + by) % 4) for i in range(4)])


def swap_cores(a):
    return lax.ppermute(a, C, [(0, 1), (1, 0)])


def gradients(queries, grad_out, keys, values, surv_index, counts):
    depth, here = lax.axis_index("rec"), lax.axis_index(X)
    kv, by_depth = pack(keys, values, queries, grad_out, surv_index, counts)
    kv = lax.all_to_all(kv, (X, Z), 0, 0, tiled=True).reshape(16 * TOK, 2 * HEAD_DIM)
    kv_other = swap_cores(kv)
    by_depth = [moved(by_depth[o], "rec", o) for o in range(4)]

    def for_x(p):
        at = lax.rem(here + p, 4)
        return jnp.concatenate([lax.dynamic_slice_in_dim(a, at, 1, axis=0) for a in by_depth], axis=0)

    qg = [moved(for_x(p), X, p) for p in range(4)]
    dq, d_own, d_other = attention(qg, kv, kv_other)
    mine = swap_cores(d_other)
    sums = (d_own + mine.astype(jnp.float32)).astype(jnp.bfloat16)
    sums = lax.all_to_all(sums.reshape(16, TOK, 2 * HEAD_DIM), (X, Z), 0, 0, tiled=True)
    dq = [moved(dq[p], X, -p) for p in range(4)]
    dq = [moved(jnp.stack([dq[p][o] for p in range(4)]), "rec", -o) for o in range(4)]
    dq = jnp.roll(jnp.stack(dq), (depth, here), (0, 1))
    query_grad = dq.reshape(HEADS, CAP, HEAD_DIM).transpose(1, 0, 2).reshape(1, CAP, HEADS * HEAD_DIM)
    key_grad, value_grad = unpack(sums)
    return query_grad, key_grad, value_grad


def solution(mesh):
    split = Mesh(mesh.devices.reshape(mesh.shape["rec"], 4, 4, 2), ("rec", X, Z, C))
    return jax.shard_map(
        gradients,
        mesh=split,
        in_specs=(
            P("rec", CTX, None),
            P("rec", CTX, None),
            P(CTX, None),
            P(CTX, None),
            P("rec", None),
            P("rec", None),
        ),
        out_specs=(P("rec", CTX, None), P(CTX, "rec"), P(CTX, "rec")),
        check_vma=False,
    )
```

```python
import math

import jax
import jax.numpy as jnp
from jax import lax
from jax.experimental import pallas as pl
from jax.experimental.pallas import tpu as pltpu
from jax.sharding import Mesh
from jax.sharding import PartitionSpec as P

HEADS = 16
HEAD_DIM = 128
CAP = 32
TOK = 128
X, Z, C = "ctx_0", "ctx_1", "ctx_2"
CTX = (X, Z, C)
GROUPS = 4
CHUNK = 512
QG_ROWS = 72
FACTOR = 1.0 / math.sqrt(HEAD_DIM)
LOG2E = 1.4426950408889634
NEG_FILL = -1e30

NT = (((1,), (1,)), ((), ()))
TN = (((0,), (0,)), ((), ()))
NN = (((1,), (0,)), ((), ()))


def dot(a, b, dims):
    return lax.dot_general(a, b, dims, preferred_element_type=jnp.float32)


def folded(a, op):
    return op(a.reshape(-1, 8, a.shape[1]), axis=0)


def group_operands(qg, x):
    src = lax.rem(lax.axis_index(X) - x + 4, 4)
    q = jnp.concatenate([qg[src, o, 0:CAP, :] for o in range(4)], axis=0)
    g = jnp.concatenate([qg[src, o, CAP : 2 * CAP, :] for o in range(4)], axis=0)
    where = sum(qg[src, o, 2 * CAP : 2 * CAP + 8, :].astype(jnp.float32) for o in range(4))
    place = 8 * x + 2 * lax.axis_index(Z) + lax.axis_index(C)
    return q, g, where[0:1, :].astype(jnp.int32) + place * TOK


def exponentials(kv, part, x, q, g, slot_pos, e_buf, w_buf):
    rows = lax.broadcasted_iota(jnp.int32, (CHUNK, TOK), 0)
    spread = rows + rows // TOK * TOK
    top = jnp.full((8, TOK), NEG_FILL, jnp.float32)
    for k in range(x + 1):
        at = slice(k * CHUNK, (k + 1) * CHUNK)
        score = dot(kv[at, 0:HEAD_DIM], q, NT)
        if k == x:
            score = jnp.where(spread + (2 * k * CHUNK + part * TOK) <= slot_pos, score, NEG_FILL)
        e_buf[at, :] = score
        top = jnp.maximum(top, folded(score, jnp.max))
    top = jnp.max(top, axis=0, keepdims=True)
    total = jnp.zeros((8, TOK), jnp.float32)
    weighted = jnp.zeros((8, TOK), jnp.float32)
    for k in range(x + 1):
        at = slice(k * CHUNK, (k + 1) * CHUNK)
        score = e_buf[at, :]
        e = jnp.exp2((score - top) * (FACTOR * LOG2E))
        if k == x:
            e = jnp.where(score > 0.5 * NEG_FILL, e, 0.0)
        dw = dot(kv[at, HEAD_DIM : 2 * HEAD_DIM], g, NT)
        e_buf[at, :] = e
        w_buf[at, :] = dw
        total = total + folded(e, jnp.sum)
        weighted = weighted + folded(e * dw, jnp.sum)
    return top, jnp.sum(total, axis=0, keepdims=True), jnp.sum(weighted, axis=0, keepdims=True)


def first_kernel(q0, q1, q2, q3, own, e_own, w_own, stats, qg):
    for p, ref in enumerate((q0, q1, q2, q3)):
        qg[p] = ref[...]
    for x in reversed(range(GROUPS)):
        q, g, slot_pos = group_operands(qg, x)
        at = pl.ds(x * (x + 1) // 2 * CHUNK, (x + 1) * CHUNK)
        part = lax.axis_index(C)
        found = exponentials(own, part, x, q, g, slot_pos, e_own.at[at], w_own.at[at])
        for n in range(3):
            stats[8 * x + n : 8 * x + n + 1, :] = found[n]


def second_kernel(*refs):
    q_in, (own, oth, e_own, w_own, stats) = refs[0:4], refs[4:9]
    q_out, (d_own, d_oth) = refs[9:13], refs[13:15]
    qg, dq, e_buf, w_buf, a_own, a_oth = refs[15:]
    for p in range(4):
        qg[p] = q_in[p][...]
    for x in reversed(range(GROUPS)):
        q, g, slot_pos = group_operands(qg, x)
        at = pl.ds(x * (x + 1) // 2 * CHUNK, (x + 1) * CHUNK)
        top, total, weighted = exponentials(oth, 1 - lax.axis_index(C), x, q, g, slot_pos, e_buf, w_buf)
        own_top, own_total, own_weighted = (stats[8 * x + n : 8 * x + n + 1, :] for n in range(3))
        joint = jnp.maximum(top, own_top)
        oth_scale = jnp.exp2((top - joint) * (FACTOR * LOG2E))
        own_scale = jnp.exp2((own_top - joint) * (FACTOR * LOG2E))
        scale = 1.0 / (total * oth_scale + own_total * own_scale)
        delta = (weighted * oth_scale + own_weighted * own_scale) * scale
        query_sum = jnp.zeros((TOK, HEAD_DIM), jnp.float32)
        for ref, acc, e_ref, w_ref, factor in (
            (oth, a_oth, e_buf, w_buf, oth_scale * scale),
            (own, a_own, e_own.at[at], w_own.at[at], own_scale * scale),
        ):
            for k in range(x + 1):
                rows = slice(k * CHUNK, (k + 1) * CHUNK)
                w = e_ref[rows, :] * factor
                ds = (w * (w_ref[rows, :] - delta)).astype(jnp.bfloat16)
                query_sum = query_sum + dot(ds, ref[rows, 0:HEAD_DIM], TN)
                key_part = dot(ds, q, NN)
                value_part = dot(w.astype(jnp.bfloat16), g, NN)
                if x == GROUPS - 1:
                    acc[rows, 0:HEAD_DIM] = key_part
                    acc[rows, HEAD_DIM : 2 * HEAD_DIM] = value_part
                else:
                    acc[rows, 0:HEAD_DIM] += key_part
                    acc[rows, HEAD_DIM : 2 * HEAD_DIM] += value_part
        src = lax.rem(lax.axis_index(X) - x + 4, 4)
        dq[src] = (query_sum * FACTOR).astype(jnp.bfloat16).reshape(4, CAP, HEAD_DIM)
    for p in range(4):
        q_out[p][...] = dq[p]
    d_own[:, 0:HEAD_DIM] = a_own[:, 0:HEAD_DIM] * FACTOR
    d_own[:, HEAD_DIM:] = a_own[:, HEAD_DIM:]
    d_oth[:, 0:HEAD_DIM] = (a_oth[:, 0:HEAD_DIM] * FACTOR).astype(jnp.bfloat16)
    d_oth[:, HEAD_DIM:] = a_oth[:, HEAD_DIM:].astype(jnp.bfloat16)


VMEM = pl.BlockSpec(memory_space=pltpu.VMEM)
HBM = pl.BlockSpec(memory_space=pltpu.HBM)
PAIRS = GROUPS * (GROUPS + 1) // 2 * CHUNK


def kernel_params(mib):
    return pltpu.CompilerParams(vmem_limit_bytes=mib * 2**20)


def attention_first(qg, own):
    return pl.pallas_call(
        first_kernel,
        out_shape=(
            jax.ShapeDtypeStruct((PAIRS, TOK), jnp.float32),
            jax.ShapeDtypeStruct((PAIRS, TOK), jnp.float32),
            jax.ShapeDtypeStruct((8 * GROUPS, TOK), jnp.float32),
        ),
        in_specs=[VMEM] * 5,
        out_specs=(VMEM,) * 3,
        scratch_shapes=[pltpu.VMEM((4, 4, QG_ROWS, HEAD_DIM), jnp.bfloat16)],
        compiler_params=kernel_params(16),
        cost_estimate=pl.CostEstimate(
            flops=2 * 2 * PAIRS * TOK * HEAD_DIM, bytes_accessed=4 * 2**20, transcendentals=PAIRS * TOK
        ),
    )(*qg, own)


def attention_second(qg, own, oth, found):
    keys = own.shape[0]
    out = pl.pallas_call(
        second_kernel,
        out_shape=(jax.ShapeDtypeStruct((4, CAP, HEAD_DIM), jnp.bfloat16),) * 4
        + (
            jax.ShapeDtypeStruct((keys, 2 * HEAD_DIM), jnp.float32),
            jax.ShapeDtypeStruct((keys, 2 * HEAD_DIM), jnp.bfloat16),
        ),
        in_specs=[VMEM] * 9,
        out_specs=(VMEM,) * 6,
        scratch_shapes=[
            pltpu.VMEM((4, 4, QG_ROWS, HEAD_DIM), jnp.bfloat16),
            pltpu.VMEM((4, 4, CAP, HEAD_DIM), jnp.bfloat16),
            pltpu.VMEM((keys, TOK), jnp.float32),
            pltpu.VMEM((keys, TOK), jnp.float32),
            pltpu.VMEM((keys, 2 * HEAD_DIM), jnp.float32),
            pltpu.VMEM((keys, 2 * HEAD_DIM), jnp.float32),
        ],
        compiler_params=kernel_params(24),
        cost_estimate=pl.CostEstimate(
            flops=2 * 8 * PAIRS * TOK * HEAD_DIM, bytes_accessed=10 * 2**20, transcendentals=PAIRS * TOK
        ),
    )(*qg, own, oth, *found)
    return out[0:4], out[4], out[5]


def pack_kernel(keys, values, queries, grad_out, surv_index, counts, kv, *rest):
    qg, (k_buf, v_buf, kv_buf, q_buf, g_buf, s_buf, c_buf, sems) = rest[0:4], rest[4:]
    depth = lax.axis_index("rec")
    ctx = lax.axis_index(X) * 8 + lax.axis_index(Z) * 2 + lax.axis_index(C)
    mine = pl.ds(pl.multiple_of(depth * 4 * HEAD_DIM, 4 * HEAD_DIM), 4 * HEAD_DIM)
    copies = [
        pltpu.make_async_copy(src, dst, sems.at[n])
        for n, (src, dst) in enumerate(
            (
                (keys.at[:, mine], k_buf),
                (values.at[:, mine], v_buf),
                (queries.at[0], q_buf),
                (grad_out.at[0], g_buf),
                (surv_index, s_buf),
                (counts, c_buf),
            )
        )
    ]
    for copy in copies:
        copy.start()
    copies[0].wait()
    copies[1].wait()
    for x in range(4):
        cols = slice(x * HEAD_DIM, (x + 1) * HEAD_DIM)
        kv_buf[x, :, 0:HEAD_DIM] = k_buf[:, cols]
        kv_buf[x, :, HEAD_DIM:] = v_buf[:, cols]
    out = [pltpu.make_async_copy(kv_buf, kv.at[:, z], sems.at[6 + z]) for z in range(4)]
    for copy in out:
        copy.start()
    for copy in copies[2:]:
        copy.wait()
    live = lax.broadcasted_iota(jnp.int32, (CAP, HEAD_DIM), 0) < c_buf[0, ctx]
    quarter = lax.rem(ctx, 4)
    near = s_buf[0:1, pl.ds(pl.multiple_of(ctx // 4 * TOK, TOK), TOK)]
    lane_group = lax.broadcasted_iota(jnp.int32, (8, TOK), 1) // CAP
    for o in range(4):
        where = pltpu.roll(jnp.broadcast_to(near, (8, TOK)), lax.rem(o - quarter + 4, 4) * CAP, 1)
        where = jnp.where(lane_group == o, where, 0).astype(jnp.float32).astype(jnp.bfloat16)
        for x in range(4):
            head = lax.rem(depth + o, 4) * 4 + x
            cols = pl.ds(pl.multiple_of(head * HEAD_DIM, HEAD_DIM), HEAD_DIM)
            qg[o][x, 0:CAP, :] = q_buf[:, cols]
            grad = jnp.where(live, g_buf[:, cols].astype(jnp.float32), 0.0)
            qg[o][x, CAP : 2 * CAP, :] = grad.astype(jnp.bfloat16)
            qg[o][x, 2 * CAP :, :] = where
    for copy in out:
        copy.wait()


def pack(keys, values, queries, grad_out, surv_index, counts):
    vmem = pl.BlockSpec(memory_space=pltpu.VMEM)
    hbm = pl.BlockSpec(memory_space=pltpu.HBM)
    out = pl.pallas_call(
        pack_kernel,
        out_shape=(jax.ShapeDtypeStruct((4, 4, TOK, 2 * HEAD_DIM), jnp.bfloat16),)
        + (jax.ShapeDtypeStruct((4, QG_ROWS, HEAD_DIM), jnp.bfloat16),) * 4,
        in_specs=[hbm] * 6,
        out_specs=(hbm,) + (vmem,) * 4,
        scratch_shapes=[
            pltpu.VMEM((TOK, 4 * HEAD_DIM), jnp.bfloat16),
            pltpu.VMEM((TOK, 4 * HEAD_DIM), jnp.bfloat16),
            pltpu.VMEM((4, TOK, 2 * HEAD_DIM), jnp.bfloat16),
            pltpu.VMEM((CAP, HEADS * HEAD_DIM), jnp.bfloat16),
            pltpu.VMEM((CAP, HEADS * HEAD_DIM), jnp.bfloat16),
            pltpu.VMEM(surv_index.shape, jnp.int32),
            pltpu.SMEM(counts.shape, jnp.int32),
            pltpu.SemaphoreType.DMA((10,)),
        ],
        compiler_params=pltpu.CompilerParams(vmem_limit_bytes=8 * 2**20),
    )(*(pltpu.with_memory_space_constraint(a, pltpu.HBM) for a in (keys, values, queries, grad_out, surv_index, counts)))
    return out[0].reshape(16, TOK, 2 * HEAD_DIM), out[1:]


def unpack_kernel(parts, key_grad, value_grad, k_buf, v_buf, sems):
    sides = ((k_buf, key_grad, 0), (v_buf, value_grad, HEAD_DIM))
    copies = []
    for n, (buf, out, at) in enumerate(sides):
        for x in range(4):
            total = sum(parts[4 * x + z, :, at : at + HEAD_DIM].astype(jnp.float32) for z in range(4))
            buf[:, x * HEAD_DIM : (x + 1) * HEAD_DIM] = total.astype(jnp.bfloat16)
        copies.append(pltpu.make_async_copy(buf, out, sems.at[n]))
        copies[n].start()
    for copy in copies:
        copy.wait()


def unpack(parts):
    out = jax.ShapeDtypeStruct((TOK, 4 * HEAD_DIM), jnp.bfloat16)
    return pl.pallas_call(
        unpack_kernel,
        out_shape=(out, out),
        in_specs=[pl.BlockSpec(memory_space=pltpu.VMEM)],
        out_specs=(pl.BlockSpec(memory_space=pl.ANY),) * 2,
        scratch_shapes=[
            pltpu.VMEM((TOK, 4 * HEAD_DIM), jnp.bfloat16),
            pltpu.VMEM((TOK, 4 * HEAD_DIM), jnp.bfloat16),
            pltpu.SemaphoreType.DMA((2,)),
        ],
        compiler_params=pltpu.CompilerParams(vmem_limit_bytes=8 * 2**20),
    )(parts)


def add_kernel(own, mine, out, buf, sems):
    copies = []
    for k in range(GROUPS):
        rows = slice(k * CHUNK, (k + 1) * CHUNK)
        buf[rows, :] = (own[rows, :] + mine[rows, :].astype(jnp.float32)).astype(jnp.bfloat16)
        copies.append(pltpu.make_async_copy(buf.at[rows], out.at[rows], sems.at[k]))
        copies[k].start()
    for copy in copies:
        copy.wait()


def added(own, mine):
    return pl.pallas_call(
        add_kernel,
        out_shape=jax.ShapeDtypeStruct(mine.shape, jnp.bfloat16),
        in_specs=[VMEM] * 2,
        out_specs=HBM,
        scratch_shapes=[pltpu.VMEM(mine.shape, jnp.bfloat16), pltpu.SemaphoreType.DMA((GROUPS,))],
        compiler_params=pltpu.CompilerParams(vmem_limit_bytes=8 * 2**20),
    )(own, mine)


def moved(a, axis, by):
    return a if by % 4 == 0 else lax.ppermute(a, axis, [(i, (i + by) % 4) for i in range(4)])


def swap_cores(a):
    return lax.ppermute(a, C, [(0, 1), (1, 0)])


def gradients(queries, grad_out, keys, values, surv_index, counts):
    depth, here = lax.axis_index("rec"), lax.axis_index(X)
    kv, by_depth = pack(keys, values, queries, grad_out, surv_index, counts)
    kv = lax.all_to_all(kv, (X, Z), 0, 0, tiled=True).reshape(16 * TOK, 2 * HEAD_DIM)
    kv_other = swap_cores(kv)
    by_depth = [moved(by_depth[o], "rec", o) for o in range(4)]

    def for_x(p):
        at = lax.rem(here + p, 4)
        return jnp.concatenate([lax.dynamic_slice_in_dim(a, at, 1, axis=0) for a in by_depth], axis=0)

    qg = [moved(for_x(p), X, p) for p in range(4)]
    found = attention_first(qg, kv)
    dq, d_own, d_other = attention_second(qg, kv, kv_other, found)
    mine = swap_cores(d_other)
    sums = added(d_own, mine)
    sums = lax.all_to_all(sums.reshape(16, TOK, 2 * HEAD_DIM), (X, Z), 0, 0, tiled=True)
    back = []
    for p in range(4):
        back.append(moved(dq[p], X, -p))
    dq = back
    dq = [moved(jnp.stack([dq[p][o] for p in range(4)]), "rec", -o) for o in range(4)]
    dq = jnp.roll(jnp.stack(dq), (depth, here), (0, 1))
    query_grad = dq.reshape(HEADS, CAP, HEAD_DIM).transpose(1, 0, 2).reshape(1, CAP, HEADS * HEAD_DIM)
    key_grad, value_grad = unpack(sums)
    return query_grad, key_grad, value_grad


def solution(mesh):
    split = Mesh(mesh.devices.reshape(mesh.shape["rec"], 4, 4, 2), ("rec", X, Z, C))
    return jax.shard_map(
        gradients,
        mesh=split,
        in_specs=(
            P("rec", CTX, None),
            P("rec", CTX, None),
            P(CTX, None),
            P(CTX, None),
            P("rec", None),
            P("rec", None),
        ),
        out_specs=(P("rec", CTX, None), P(CTX, "rec"), P(CTX, "rec")),
        check_vma=False,
    )
```

```python
import math

import jax
import jax.numpy as jnp
from jax import lax
from jax.experimental import pallas as pl
from jax.experimental.pallas import tpu as pltpu
from jax.sharding import Mesh
from jax.sharding import PartitionSpec as P

HEADS = 16
HEAD_DIM = 128
CAP = 32
TOK = 128
X, Z, C = "ctx_0", "ctx_1", "ctx_2"
CTX = (X, Z, C)
GROUPS = 4
CHUNK = 512
QG_ROWS = 72
FACTOR = 1.0 / math.sqrt(HEAD_DIM)
LOG2E = 1.4426950408889634
NEG_FILL = -1e30

NT = (((1,), (1,)), ((), ()))
TN = (((0,), (0,)), ((), ()))
NN = (((1,), (0,)), ((), ()))


def dot(a, b, dims):
    return lax.dot_general(a, b, dims, preferred_element_type=jnp.float32)


def folded(a, op):
    return op(a.reshape(-1, 8, a.shape[1]), axis=0)


def group_operands(qg, x):
    src = lax.rem(lax.axis_index(X) - x + 4, 4)
    q = jnp.concatenate([qg[src, o, 0:CAP, :] for o in range(4)], axis=0)
    g = jnp.concatenate([qg[src, o, CAP : 2 * CAP, :] for o in range(4)], axis=0)
    where = sum(qg[src, o, 2 * CAP : 2 * CAP + 8, :].astype(jnp.float32) for o in range(4))
    place = 8 * x + 2 * lax.axis_index(Z) + lax.axis_index(C)
    return q, g, where[0:1, :].astype(jnp.int32) + place * TOK


def exponentials(kv, part, x, q, g, slot_pos, e_buf, w_buf):
    rows = lax.broadcasted_iota(jnp.int32, (CHUNK, TOK), 0)
    spread = rows + rows // TOK * TOK
    top = jnp.full((8, TOK), NEG_FILL, jnp.float32)
    for k in range(x + 1):
        at = slice(k * CHUNK, (k + 1) * CHUNK)
        score = dot(kv[at, 0:HEAD_DIM], q, NT)
        if k == x:
            score = jnp.where(spread + (2 * k * CHUNK + part * TOK) <= slot_pos, score, NEG_FILL)
        e_buf[at, :] = score
        top = jnp.maximum(top, folded(score, jnp.max))
    top = jnp.max(top, axis=0, keepdims=True)
    total = jnp.zeros((8, TOK), jnp.float32)
    weighted = jnp.zeros((8, TOK), jnp.float32)
    for k in range(x + 1):
        at = slice(k * CHUNK, (k + 1) * CHUNK)
        score = e_buf[at, :]
        e = jnp.exp2((score - top) * (FACTOR * LOG2E))
        if k == x:
            e = jnp.where(score > 0.5 * NEG_FILL, e, 0.0)
        dw = dot(kv[at, HEAD_DIM : 2 * HEAD_DIM], g, NT)
        e_buf[at, :] = e
        w_buf[at, :] = dw
        total = total + folded(e, jnp.sum)
        weighted = weighted + folded(e * dw, jnp.sum)
    return top, jnp.sum(total, axis=0, keepdims=True), jnp.sum(weighted, axis=0, keepdims=True)


def first_kernel(q0, q1, q2, q3, own, e_own, w_own, stats, qg):
    for p, ref in enumerate((q0, q1, q2, q3)):
        qg[p] = ref[...]
    for x in reversed(range(GROUPS)):
        q, g, slot_pos = group_operands(qg, x)
        at = pl.ds(x * (x + 1) // 2 * CHUNK, (x + 1) * CHUNK)
        part = lax.axis_index(C)
        found = exponentials(own, part, x, q, g, slot_pos, e_own.at[at], w_own.at[at])
        for n in range(3):
            stats[8 * x + n : 8 * x + n + 1, :] = found[n]


def second_kernel(*refs):
    q_in, (own, oth, e_own, w_own, stats) = refs[0:4], refs[4:9]
    q_out, (d_own, d_oth) = refs[9:13], refs[13:15]
    qg, dq, e_buf, w_buf, a_own, a_oth = refs[15:]
    for p in range(4):
        qg[p] = q_in[p][...]
    for x in reversed(range(GROUPS)):
        q, g, slot_pos = group_operands(qg, x)
        at = pl.ds(x * (x + 1) // 2 * CHUNK, (x + 1) * CHUNK)
        top, total, weighted = exponentials(oth, 1 - lax.axis_index(C), x, q, g, slot_pos, e_buf, w_buf)
        own_top, own_total, own_weighted = (stats[8 * x + n : 8 * x + n + 1, :] for n in range(3))
        joint = jnp.maximum(top, own_top)
        oth_scale = jnp.exp2((top - joint) * (FACTOR * LOG2E))
        own_scale = jnp.exp2((own_top - joint) * (FACTOR * LOG2E))
        scale = 1.0 / (total * oth_scale + own_total * own_scale)
        delta = (weighted * oth_scale + own_weighted * own_scale) * scale
        query_sum = jnp.zeros((TOK, HEAD_DIM), jnp.float32)
        for ref, acc, e_ref, w_ref, factor in (
            (oth, a_oth, e_buf, w_buf, oth_scale * scale),
            (own, a_own, e_own.at[at], w_own.at[at], own_scale * scale),
        ):
            for k in range(x + 1):
                rows = slice(k * CHUNK, (k + 1) * CHUNK)
                w = e_ref[rows, :] * factor
                ds = (w * (w_ref[rows, :] - delta)).astype(jnp.bfloat16)
                query_sum = query_sum + dot(ds, ref[rows, 0:HEAD_DIM], TN)
                key_part = dot(ds, q, NN)
                value_part = dot(w.astype(jnp.bfloat16), g, NN)
                if x == GROUPS - 1:
                    acc[rows, 0:HEAD_DIM] = key_part
                    acc[rows, HEAD_DIM : 2 * HEAD_DIM] = value_part
                else:
                    acc[rows, 0:HEAD_DIM] += key_part
                    acc[rows, HEAD_DIM : 2 * HEAD_DIM] += value_part
        src = lax.rem(lax.axis_index(X) - x + 4, 4)
        query_out = (query_sum * FACTOR).astype(jnp.bfloat16)
        for o in range(4):
            dq[o, src] = query_out[CAP * o : CAP * (o + 1), :]
    for o in range(4):
        q_out[o][...] = dq[o]
    d_own[:, 0:HEAD_DIM] = a_own[:, 0:HEAD_DIM] * FACTOR
    d_own[:, HEAD_DIM:] = a_own[:, HEAD_DIM:]
    d_oth[:, 0:HEAD_DIM] = (a_oth[:, 0:HEAD_DIM] * FACTOR).astype(jnp.bfloat16)
    d_oth[:, HEAD_DIM:] = a_oth[:, HEAD_DIM:].astype(jnp.bfloat16)


VMEM = pl.BlockSpec(memory_space=pltpu.VMEM)
HBM = pl.BlockSpec(memory_space=pltpu.HBM)
PAIRS = GROUPS * (GROUPS + 1) // 2 * CHUNK


def kernel_params(mib):
    return pltpu.CompilerParams(vmem_limit_bytes=mib * 2**20)


def attention_first(qg, own):
    return pl.pallas_call(
        first_kernel,
        out_shape=(
            jax.ShapeDtypeStruct((PAIRS, TOK), jnp.float32),
            jax.ShapeDtypeStruct((PAIRS, TOK), jnp.float32),
            jax.ShapeDtypeStruct((8 * GROUPS, TOK), jnp.float32),
        ),
        in_specs=[VMEM] * 5,
        out_specs=(VMEM,) * 3,
        scratch_shapes=[pltpu.VMEM((4, 4, QG_ROWS, HEAD_DIM), jnp.bfloat16)],
        compiler_params=kernel_params(16),
        cost_estimate=pl.CostEstimate(
            flops=2 * 2 * PAIRS * TOK * HEAD_DIM, bytes_accessed=4 * 2**20, transcendentals=PAIRS * TOK
        ),
    )(*qg, own)


def attention_second(qg, own, oth, found):
    keys = own.shape[0]
    out = pl.pallas_call(
        second_kernel,
        out_shape=(jax.ShapeDtypeStruct((4, CAP, HEAD_DIM), jnp.bfloat16),) * 4
        + (
            jax.ShapeDtypeStruct((keys, 2 * HEAD_DIM), jnp.float32),
            jax.ShapeDtypeStruct((keys, 2 * HEAD_DIM), jnp.bfloat16),
        ),
        in_specs=[VMEM] * 9,
        out_specs=(VMEM,) * 6,
        scratch_shapes=[
            pltpu.VMEM((4, 4, QG_ROWS, HEAD_DIM), jnp.bfloat16),
            pltpu.VMEM((4, 4, CAP, HEAD_DIM), jnp.bfloat16),
            pltpu.VMEM((keys, TOK), jnp.float32),
            pltpu.VMEM((keys, TOK), jnp.float32),
            pltpu.VMEM((keys, 2 * HEAD_DIM), jnp.float32),
            pltpu.VMEM((keys, 2 * HEAD_DIM), jnp.float32),
        ],
        compiler_params=kernel_params(24),
        cost_estimate=pl.CostEstimate(
            flops=2 * 8 * PAIRS * TOK * HEAD_DIM, bytes_accessed=10 * 2**20, transcendentals=PAIRS * TOK
        ),
    )(*qg, own, oth, *found)
    return out[0:4], out[4], out[5]


def pack_kernel(keys, values, queries, grad_out, surv_index, counts, kv, *rest):
    qg, (k_buf, v_buf, kv_buf, q_buf, g_buf, s_buf, c_buf, sems) = rest[0:4], rest[4:]
    depth = lax.axis_index("rec")
    ctx = lax.axis_index(X) * 8 + lax.axis_index(Z) * 2 + lax.axis_index(C)
    mine = pl.ds(pl.multiple_of(depth * 4 * HEAD_DIM, 4 * HEAD_DIM), 4 * HEAD_DIM)
    copies = [
        pltpu.make_async_copy(src, dst, sems.at[n])
        for n, (src, dst) in enumerate(
            (
                (keys.at[:, mine], k_buf),
                (values.at[:, mine], v_buf),
                (queries.at[0], q_buf),
                (grad_out.at[0], g_buf),
                (surv_index, s_buf),
                (counts, c_buf),
            )
        )
    ]
    for copy in copies:
        copy.start()
    copies[0].wait()
    copies[1].wait()
    for x in range(4):
        cols = slice(x * HEAD_DIM, (x + 1) * HEAD_DIM)
        kv_buf[x, :, 0:HEAD_DIM] = k_buf[:, cols]
        kv_buf[x, :, HEAD_DIM:] = v_buf[:, cols]
    out = [pltpu.make_async_copy(kv_buf, kv.at[:, z], sems.at[6 + z]) for z in range(4)]
    for copy in out:
        copy.start()
    for copy in copies[2:]:
        copy.wait()
    live = lax.broadcasted_iota(jnp.int32, (CAP, HEAD_DIM), 0) < c_buf[0, ctx]
    quarter = lax.rem(ctx, 4)
    near = s_buf[0:1, pl.ds(pl.multiple_of(ctx // 4 * TOK, TOK), TOK)]
    lane_group = lax.broadcasted_iota(jnp.int32, (8, TOK), 1) // CAP
    for o in range(4):
        where = pltpu.roll(jnp.broadcast_to(near, (8, TOK)), lax.rem(o - quarter + 4, 4) * CAP, 1)
        where = jnp.where(lane_group == o, where, 0).astype(jnp.float32).astype(jnp.bfloat16)
        for x in range(4):
            head = lax.rem(depth + o, 4) * 4 + x
            cols = pl.ds(pl.multiple_of(head * HEAD_DIM, HEAD_DIM), HEAD_DIM)
            qg[o][x, 0:CAP, :] = q_buf[:, cols]
            grad = jnp.where(live, g_buf[:, cols].astype(jnp.float32), 0.0)
            qg[o][x, CAP : 2 * CAP, :] = grad.astype(jnp.bfloat16)
            qg[o][x, 2 * CAP :, :] = where
    for copy in out:
        copy.wait()


def pack(keys, values, queries, grad_out, surv_index, counts):
    vmem = pl.BlockSpec(memory_space=pltpu.VMEM)
    hbm = pl.BlockSpec(memory_space=pltpu.HBM)
    out = pl.pallas_call(
        pack_kernel,
        out_shape=(jax.ShapeDtypeStruct((4, 4, TOK, 2 * HEAD_DIM), jnp.bfloat16),)
        + (jax.ShapeDtypeStruct((4, QG_ROWS, HEAD_DIM), jnp.bfloat16),) * 4,
        in_specs=[hbm] * 6,
        out_specs=(hbm,) + (vmem,) * 4,
        scratch_shapes=[
            pltpu.VMEM((TOK, 4 * HEAD_DIM), jnp.bfloat16),
            pltpu.VMEM((TOK, 4 * HEAD_DIM), jnp.bfloat16),
            pltpu.VMEM((4, TOK, 2 * HEAD_DIM), jnp.bfloat16),
            pltpu.VMEM((CAP, HEADS * HEAD_DIM), jnp.bfloat16),
            pltpu.VMEM((CAP, HEADS * HEAD_DIM), jnp.bfloat16),
            pltpu.VMEM(surv_index.shape, jnp.int32),
            pltpu.SMEM(counts.shape, jnp.int32),
            pltpu.SemaphoreType.DMA((10,)),
        ],
        compiler_params=pltpu.CompilerParams(vmem_limit_bytes=8 * 2**20),
    )(*(pltpu.with_memory_space_constraint(a, pltpu.HBM) for a in (keys, values, queries, grad_out, surv_index, counts)))
    return out[0].reshape(16, TOK, 2 * HEAD_DIM), out[1:]


def finish_kernel(parts, q0, q1, q2, q3, key_grad, value_grad, query_grad, k_buf, v_buf, q_buf, sems):
    copies = []
    for n, (buf, out, at) in enumerate(((k_buf, key_grad, 0), (v_buf, value_grad, HEAD_DIM))):
        for x in range(4):
            total = sum(parts[4 * x + z, :, at : at + HEAD_DIM].astype(jnp.float32) for z in range(4))
            buf[:, x * HEAD_DIM : (x + 1) * HEAD_DIM] = total.astype(jnp.bfloat16)
        copies.append(pltpu.make_async_copy(buf, out, sems.at[n]))
        copies[n].start()
    depth, here = lax.axis_index("rec"), lax.axis_index(X)
    for p, ref in enumerate((q0, q1, q2, q3)):
        for o in range(4):
            head = lax.rem(depth + o, 4) * 4 + lax.rem(here + p, 4)
            q_buf[:, pl.ds(pl.multiple_of(head * HEAD_DIM, HEAD_DIM), HEAD_DIM)] = ref[o]
    copies.append(pltpu.make_async_copy(q_buf, query_grad.at[0], sems.at[2]))
    copies[2].start()
    for copy in copies:
        copy.wait()


def finish(parts, dq):
    out = jax.ShapeDtypeStruct((TOK, 4 * HEAD_DIM), jnp.bfloat16)
    return pl.pallas_call(
        finish_kernel,
        out_shape=(out, out, jax.ShapeDtypeStruct((1, CAP, HEADS * HEAD_DIM), jnp.bfloat16)),
        in_specs=[VMEM] * 5,
        out_specs=(pl.BlockSpec(memory_space=pl.ANY),) * 3,
        scratch_shapes=[
            pltpu.VMEM((TOK, 4 * HEAD_DIM), jnp.bfloat16),
            pltpu.VMEM((TOK, 4 * HEAD_DIM), jnp.bfloat16),
            pltpu.VMEM((CAP, HEADS * HEAD_DIM), jnp.bfloat16),
            pltpu.SemaphoreType.DMA((3,)),
        ],
        compiler_params=pltpu.CompilerParams(vmem_limit_bytes=8 * 2**20),
    )(parts, *dq)


def add_kernel(own, mine, out, buf, sems):
    copies = []
    for k in range(GROUPS):
        rows = slice(k * CHUNK, (k + 1) * CHUNK)
        buf[rows, :] = (own[rows, :] + mine[rows, :].astype(jnp.float32)).astype(jnp.bfloat16)
        copies.append(pltpu.make_async_copy(buf.at[rows], out.at[rows], sems.at[k]))
        copies[k].start()
    for copy in copies:
        copy.wait()


def added(own, mine):
    return pl.pallas_call(
        add_kernel,
        out_shape=jax.ShapeDtypeStruct(mine.shape, jnp.bfloat16),
        in_specs=[VMEM] * 2,
        out_specs=HBM,
        scratch_shapes=[pltpu.VMEM(mine.shape, jnp.bfloat16), pltpu.SemaphoreType.DMA((GROUPS,))],
        compiler_params=pltpu.CompilerParams(vmem_limit_bytes=8 * 2**20),
    )(own, mine)


def moved(a, axis, by):
    return a if by % 4 == 0 else lax.ppermute(a, axis, [(i, (i + by) % 4) for i in range(4)])


def swap_cores(a):
    return lax.ppermute(a, C, [(0, 1), (1, 0)])


def gradients(queries, grad_out, keys, values, surv_index, counts):
    here = lax.axis_index(X)
    kv, by_depth = pack(keys, values, queries, grad_out, surv_index, counts)
    kv = lax.all_to_all(kv, (X, Z), 0, 0, tiled=True).reshape(16 * TOK, 2 * HEAD_DIM)
    kv_other = swap_cores(kv)
    by_depth = [moved(by_depth[o], "rec", o) for o in range(4)]

    def for_x(p):
        at = lax.rem(here + p, 4)
        return jnp.concatenate([lax.dynamic_slice_in_dim(a, at, 1, axis=0) for a in by_depth], axis=0)

    qg = [moved(for_x(p), X, p) for p in range(4)]
    found = attention_first(qg, kv)
    dq, d_own, d_other = attention_second(qg, kv, kv_other, found)
    mine = swap_cores(d_other)
    sums = added(d_own, mine)
    sums = lax.all_to_all(sums.reshape(16, TOK, 2 * HEAD_DIM), (X, Z), 0, 0, tiled=True)
    dq = [moved(dq[o], "rec", -o) for o in range(4)]
    dq = [moved(jnp.stack([dq[o][p] for o in range(4)]), X, -p) for p in range(4)]
    key_grad, value_grad, query_grad = finish(sums, dq)
    return query_grad, key_grad, value_grad


def solution(mesh):
    split = Mesh(mesh.devices.reshape(mesh.shape["rec"], 4, 4, 2), ("rec", X, Z, C))
    return jax.shard_map(
        gradients,
        mesh=split,
        in_specs=(
            P("rec", CTX, None),
            P("rec", CTX, None),
            P(CTX, None),
            P(CTX, None),
            P("rec", None),
            P("rec", None),
        ),
        out_specs=(P("rec", CTX, None), P(CTX, "rec"), P(CTX, "rec")),
        check_vma=False,
    )
```

```python
import math

import jax
import jax.numpy as jnp
from jax import lax
from jax.experimental import pallas as pl
from jax.experimental.pallas import tpu as pltpu
from jax.sharding import Mesh
from jax.sharding import PartitionSpec as P

HEADS = 16
HEAD_DIM = 128
CAP = 32
TOK = 128
X, Z, C = "ctx_0", "ctx_1", "ctx_2"
CTX = (X, Z, C)
GROUPS = 4
CHUNK = 512
QG_ROWS = 72
FACTOR = 1.0 / math.sqrt(HEAD_DIM)
LOG2E = 1.4426950408889634
NEG_FILL = -1e30

NT = (((1,), (1,)), ((), ()))
TN = (((0,), (0,)), ((), ()))
NN = (((1,), (0,)), ((), ()))


def dot(a, b, dims):
    return lax.dot_general(a, b, dims, preferred_element_type=jnp.float32)


def folded(a, op):
    return op(a.reshape(-1, 8, a.shape[1]), axis=0)


def group_operands(qg, x):
    src = lax.rem(lax.axis_index(X) - x + 4, 4)
    q = jnp.concatenate([qg[src, o, 0:CAP, :] for o in range(4)], axis=0)
    g = jnp.concatenate([qg[src, o, CAP : 2 * CAP, :] for o in range(4)], axis=0)
    where = sum(qg[src, o, 2 * CAP : 2 * CAP + 8, :].astype(jnp.float32) for o in range(4))
    place = 8 * x + 2 * lax.axis_index(Z) + lax.axis_index(C)
    return q, g, where[0:1, :].astype(jnp.int32) + place * TOK


def exponentials(kv, part, x, q, g, slot_pos, e_buf, w_buf):
    rows = lax.broadcasted_iota(jnp.int32, (CHUNK, TOK), 0)
    spread = rows + rows // TOK * TOK
    top = jnp.full((8, TOK), NEG_FILL, jnp.float32)
    for k in range(x + 1):
        at = slice(k * CHUNK, (k + 1) * CHUNK)
        score = dot(kv[at, 0:HEAD_DIM], q, NT)
        if k == x:
            score = jnp.where(spread + (2 * k * CHUNK + part * TOK) <= slot_pos, score, NEG_FILL)
        e_buf[at, :] = score
        top = jnp.maximum(top, folded(score, jnp.max))
    top = jnp.max(top, axis=0, keepdims=True)
    total = jnp.zeros((8, TOK), jnp.float32)
    weighted = jnp.zeros((8, TOK), jnp.float32)
    for k in range(x + 1):
        at = slice(k * CHUNK, (k + 1) * CHUNK)
        score = e_buf[at, :]
        e = jnp.exp2((score - top) * (FACTOR * LOG2E))
        if k == x:
            e = jnp.where(score > 0.5 * NEG_FILL, e, 0.0)
        dw = dot(kv[at, HEAD_DIM : 2 * HEAD_DIM], g, NT)
        e_buf[at, :] = e
        w_buf[at, :] = dw
        total = total + folded(e, jnp.sum)
        weighted = weighted + folded(e * dw, jnp.sum)
    return top, jnp.sum(total, axis=0, keepdims=True), jnp.sum(weighted, axis=0, keepdims=True)


def first_kernel(q0, q1, q2, q3, own, e_own, w_own, stats, qg):
    for p, ref in enumerate((q0, q1, q2, q3)):
        qg[p] = ref[...]
    for x in reversed(range(GROUPS)):
        q, g, slot_pos = group_operands(qg, x)
        at = pl.ds(x * (x + 1) // 2 * CHUNK, (x + 1) * CHUNK)
        part = lax.axis_index(C)
        found = exponentials(own, part, x, q, g, slot_pos, e_own.at[at], w_own.at[at])
        for n in range(3):
            stats[8 * x + n : 8 * x + n + 1, :] = found[n]


def second_kernel(*refs):
    q_in, (oth, own, e_own, w_own, stats) = refs[0:4], refs[4:9]
    q_out, (d_oth, ds_own, wb_own) = refs[9:13], refs[13:16]
    qg, dq, e_buf, w_buf, acc = refs[16:]
    for p in range(4):
        qg[p] = q_in[p][...]
    for x in reversed(range(GROUPS)):
        q, g, slot_pos = group_operands(qg, x)
        first = x * (x + 1) // 2 * CHUNK
        top, total, weighted = exponentials(oth, 1 - lax.axis_index(C), x, q, g, slot_pos, e_buf, w_buf)
        own_top, own_total, own_weighted = (stats[8 * x + n : 8 * x + n + 1, :] for n in range(3))
        joint = jnp.maximum(top, own_top)
        oth_scale = jnp.exp2((top - joint) * (FACTOR * LOG2E))
        own_scale = jnp.exp2((own_top - joint) * (FACTOR * LOG2E))
        scale = 1.0 / (total * oth_scale + own_total * own_scale)
        delta = (weighted * oth_scale + own_weighted * own_scale) * scale
        query_sum = jnp.zeros((TOK, HEAD_DIM), jnp.float32)
        for k in range(x + 1):
            rows = slice(k * CHUNK, (k + 1) * CHUNK)
            w = e_buf[rows, :] * (oth_scale * scale)
            ds = (w * (w_buf[rows, :] - delta)).astype(jnp.bfloat16)
            query_sum = query_sum + dot(ds, oth[rows, 0:HEAD_DIM], TN)
            key_part = dot(ds, q, NN)
            value_part = dot(w.astype(jnp.bfloat16), g, NN)
            if x == GROUPS - 1:
                acc[rows, 0:HEAD_DIM] = key_part
                acc[rows, HEAD_DIM : 2 * HEAD_DIM] = value_part
            else:
                acc[rows, 0:HEAD_DIM] += key_part
                acc[rows, HEAD_DIM : 2 * HEAD_DIM] += value_part
        for k in range(x + 1):
            at = slice(first + k * CHUNK, first + (k + 1) * CHUNK)
            w = e_own[at, :] * (own_scale * scale)
            ds = (w * (w_own[at, :] - delta)).astype(jnp.bfloat16)
            query_sum = query_sum + dot(ds, own[k * CHUNK : (k + 1) * CHUNK, 0:HEAD_DIM], TN)
            ds_own[at, :] = ds
            wb_own[at, :] = w.astype(jnp.bfloat16)
        src = lax.rem(lax.axis_index(X) - x + 4, 4)
        query_out = (query_sum * FACTOR).astype(jnp.bfloat16)
        for o in range(4):
            dq[o, src] = query_out[CAP * o : CAP * (o + 1), :]
    for o in range(4):
        q_out[o][...] = dq[o]
    d_oth[:, 0:HEAD_DIM] = (acc[:, 0:HEAD_DIM] * FACTOR).astype(jnp.bfloat16)
    d_oth[:, HEAD_DIM:] = acc[:, HEAD_DIM:].astype(jnp.bfloat16)


def third_kernel(q0, q1, q2, q3, ds_own, wb_own, d_own, qg):
    for p, ref in enumerate((q0, q1, q2, q3)):
        qg[p] = ref[...]
    for x in reversed(range(GROUPS)):
        q, g, _ = group_operands(qg, x)
        for k in range(x + 1):
            rows = slice(k * CHUNK, (k + 1) * CHUNK)
            at = slice(x * (x + 1) // 2 * CHUNK + k * CHUNK, x * (x + 1) // 2 * CHUNK + (k + 1) * CHUNK)
            key_part = dot(ds_own[at, :], q, NN)
            value_part = dot(wb_own[at, :], g, NN)
            if x == GROUPS - 1:
                d_own[rows, 0:HEAD_DIM] = key_part
                d_own[rows, HEAD_DIM : 2 * HEAD_DIM] = value_part
            else:
                d_own[rows, 0:HEAD_DIM] += key_part
                d_own[rows, HEAD_DIM : 2 * HEAD_DIM] += value_part


VMEM = pl.BlockSpec(memory_space=pltpu.VMEM)
HBM = pl.BlockSpec(memory_space=pltpu.HBM)
PAIRS = GROUPS * (GROUPS + 1) // 2 * CHUNK


def kernel_params(mib):
    return pltpu.CompilerParams(vmem_limit_bytes=mib * 2**20)


def attention_first(qg, own):
    return pl.pallas_call(
        first_kernel,
        out_shape=(
            jax.ShapeDtypeStruct((PAIRS, TOK), jnp.float32),
            jax.ShapeDtypeStruct((PAIRS, TOK), jnp.float32),
            jax.ShapeDtypeStruct((8 * GROUPS, TOK), jnp.float32),
        ),
        in_specs=[VMEM] * 5,
        out_specs=(VMEM,) * 3,
        scratch_shapes=[pltpu.VMEM((4, 4, QG_ROWS, HEAD_DIM), jnp.bfloat16)],
        compiler_params=kernel_params(16),
        cost_estimate=pl.CostEstimate(
            flops=2 * 2 * PAIRS * TOK * HEAD_DIM, bytes_accessed=4 * 2**20, transcendentals=PAIRS * TOK
        ),
    )(*qg, own)


def attention_second(qg, own, oth, found):
    keys = own.shape[0]
    out = pl.pallas_call(
        second_kernel,
        out_shape=(jax.ShapeDtypeStruct((4, CAP, HEAD_DIM), jnp.bfloat16),) * 4
        + (
            jax.ShapeDtypeStruct((keys, 2 * HEAD_DIM), jnp.bfloat16),
            jax.ShapeDtypeStruct((PAIRS, TOK), jnp.bfloat16),
            jax.ShapeDtypeStruct((PAIRS, TOK), jnp.bfloat16),
        ),
        in_specs=[VMEM] * 9,
        out_specs=(VMEM,) * 7,
        scratch_shapes=[
            pltpu.VMEM((4, 4, QG_ROWS, HEAD_DIM), jnp.bfloat16),
            pltpu.VMEM((4, 4, CAP, HEAD_DIM), jnp.bfloat16),
            pltpu.VMEM((keys, TOK), jnp.float32),
            pltpu.VMEM((keys, TOK), jnp.float32),
            pltpu.VMEM((keys, 2 * HEAD_DIM), jnp.float32),
        ],
        compiler_params=kernel_params(20),
        cost_estimate=pl.CostEstimate(
            flops=2 * 6 * PAIRS * TOK * HEAD_DIM, bytes_accessed=10 * 2**20, transcendentals=PAIRS * TOK
        ),
    )(*qg, oth, own, *found)
    return out[0:4], out[4], out[5:7]


def attention_third(qg, products):
    return pl.pallas_call(
        third_kernel,
        out_shape=jax.ShapeDtypeStruct((GROUPS * CHUNK, 2 * HEAD_DIM), jnp.float32),
        in_specs=[VMEM] * 6,
        out_specs=VMEM,
        scratch_shapes=[pltpu.VMEM((4, 4, QG_ROWS, HEAD_DIM), jnp.bfloat16)],
        compiler_params=kernel_params(12),
        cost_estimate=pl.CostEstimate(
            flops=2 * 2 * PAIRS * TOK * HEAD_DIM, bytes_accessed=5 * 2**20, transcendentals=0
        ),
    )(*qg, *products)


def pack_kernel(keys, values, queries, grad_out, surv_index, counts, kv, *rest):
    qg, (k_buf, v_buf, kv_buf, q_buf, g_buf, s_buf, c_buf, sems) = rest[0:4], rest[4:]
    depth = lax.axis_index("rec")
    ctx = lax.axis_index(X) * 8 + lax.axis_index(Z) * 2 + lax.axis_index(C)
    mine = pl.ds(pl.multiple_of(depth * 4 * HEAD_DIM, 4 * HEAD_DIM), 4 * HEAD_DIM)
    copies = [
        pltpu.make_async_copy(src, dst, sems.at[n])
        for n, (src, dst) in enumerate(
            (
                (keys.at[:, mine], k_buf),
                (values.at[:, mine], v_buf),
                (queries.at[0], q_buf),
                (grad_out.at[0], g_buf),
                (surv_index, s_buf),
                (counts, c_buf),
            )
        )
    ]
    for copy in copies:
        copy.start()
    copies[0].wait()
    copies[1].wait()
    for x in range(4):
        cols = slice(x * HEAD_DIM, (x + 1) * HEAD_DIM)
        kv_buf[x, :, 0:HEAD_DIM] = k_buf[:, cols]
        kv_buf[x, :, HEAD_DIM:] = v_buf[:, cols]
    out = [pltpu.make_async_copy(kv_buf, kv.at[:, z], sems.at[6 + z]) for z in range(4)]
    for copy in out:
        copy.start()
    for copy in copies[2:]:
        copy.wait()
    live = lax.broadcasted_iota(jnp.int32, (CAP, HEAD_DIM), 0) < c_buf[0, ctx]
    quarter = lax.rem(ctx, 4)
    near = s_buf[0:1, pl.ds(pl.multiple_of(ctx // 4 * TOK, TOK), TOK)]
    lane_group = lax.broadcasted_iota(jnp.int32, (8, TOK), 1) // CAP
    for o in range(4):
        where = pltpu.roll(jnp.broadcast_to(near, (8, TOK)), lax.rem(o - quarter + 4, 4) * CAP, 1)
        where = jnp.where(lane_group == o, where, 0).astype(jnp.float32).astype(jnp.bfloat16)
        for x in range(4):
            head = lax.rem(depth + o, 4) * 4 + x
            cols = pl.ds(pl.multiple_of(head * HEAD_DIM, HEAD_DIM), HEAD_DIM)
            qg[o][x, 0:CAP, :] = q_buf[:, cols]
            grad = jnp.where(live, g_buf[:, cols].astype(jnp.float32), 0.0)
            qg[o][x, CAP : 2 * CAP, :] = grad.astype(jnp.bfloat16)
            qg[o][x, 2 * CAP :, :] = where
    for copy in out:
        copy.wait()


def pack(keys, values, queries, grad_out, surv_index, counts):
    vmem = pl.BlockSpec(memory_space=pltpu.VMEM)
    hbm = pl.BlockSpec(memory_space=pltpu.HBM)
    out = pl.pallas_call(
        pack_kernel,
        out_shape=(jax.ShapeDtypeStruct((4, 4, TOK, 2 * HEAD_DIM), jnp.bfloat16),)
        + (jax.ShapeDtypeStruct((4, QG_ROWS, HEAD_DIM), jnp.bfloat16),) * 4,
        in_specs=[hbm] * 6,
        out_specs=(hbm,) + (vmem,) * 4,
        scratch_shapes=[
            pltpu.VMEM((TOK, 4 * HEAD_DIM), jnp.bfloat16),
            pltpu.VMEM((TOK, 4 * HEAD_DIM), jnp.bfloat16),
            pltpu.VMEM((4, TOK, 2 * HEAD_DIM), jnp.bfloat16),
            pltpu.VMEM((CAP, HEADS * HEAD_DIM), jnp.bfloat16),
            pltpu.VMEM((CAP, HEADS * HEAD_DIM), jnp.bfloat16),
            pltpu.VMEM(surv_index.shape, jnp.int32),
            pltpu.SMEM(counts.shape, jnp.int32),
            pltpu.SemaphoreType.DMA((10,)),
        ],
        compiler_params=pltpu.CompilerParams(vmem_limit_bytes=8 * 2**20),
    )(*(pltpu.with_memory_space_constraint(a, pltpu.HBM) for a in (keys, values, queries, grad_out, surv_index, counts)))
    return out[0].reshape(16, TOK, 2 * HEAD_DIM), out[1:]


def finish_kernel(parts, q0, q1, q2, q3, key_grad, value_grad, query_grad, k_buf, v_buf, q_buf, sems):
    copies = []
    for n, (buf, out, at) in enumerate(((k_buf, key_grad, 0), (v_buf, value_grad, HEAD_DIM))):
        for x in range(4):
            total = sum(parts[4 * x + z, :, at : at + HEAD_DIM].astype(jnp.float32) for z in range(4))
            buf[:, x * HEAD_DIM : (x + 1) * HEAD_DIM] = total.astype(jnp.bfloat16)
        copies.append(pltpu.make_async_copy(buf, out, sems.at[n]))
        copies[n].start()
    depth, here = lax.axis_index("rec"), lax.axis_index(X)
    for p, ref in enumerate((q0, q1, q2, q3)):
        for o in range(4):
            head = lax.rem(depth + o, 4) * 4 + lax.rem(here + p, 4)
            q_buf[:, pl.ds(pl.multiple_of(head * HEAD_DIM, HEAD_DIM), HEAD_DIM)] = ref[o]
    copies.append(pltpu.make_async_copy(q_buf, query_grad.at[0], sems.at[2]))
    copies[2].start()
    for copy in copies:
        copy.wait()


def finish(parts, dq):
    out = jax.ShapeDtypeStruct((TOK, 4 * HEAD_DIM), jnp.bfloat16)
    return pl.pallas_call(
        finish_kernel,
        out_shape=(out, out, jax.ShapeDtypeStruct((1, CAP, HEADS * HEAD_DIM), jnp.bfloat16)),
        in_specs=[VMEM] * 5,
        out_specs=(pl.BlockSpec(memory_space=pl.ANY),) * 3,
        scratch_shapes=[
            pltpu.VMEM((TOK, 4 * HEAD_DIM), jnp.bfloat16),
            pltpu.VMEM((TOK, 4 * HEAD_DIM), jnp.bfloat16),
            pltpu.VMEM((CAP, HEADS * HEAD_DIM), jnp.bfloat16),
            pltpu.SemaphoreType.DMA((3,)),
        ],
        compiler_params=pltpu.CompilerParams(vmem_limit_bytes=8 * 2**20),
    )(parts, *dq)


def add_kernel(own, mine, out, buf, sems):
    copies = []
    for k in range(GROUPS):
        rows = slice(k * CHUNK, (k + 1) * CHUNK)
        other = mine[rows, :].astype(jnp.float32)
        buf[rows, 0:HEAD_DIM] = (own[rows, 0:HEAD_DIM] * FACTOR + other[:, 0:HEAD_DIM]).astype(jnp.bfloat16)
        buf[rows, HEAD_DIM:] = (own[rows, HEAD_DIM:] + other[:, HEAD_DIM:]).astype(jnp.bfloat16)
        copies.append(pltpu.make_async_copy(buf.at[rows], out.at[rows], sems.at[k]))
        copies[k].start()
    for copy in copies:
        copy.wait()


def added(own, mine):
    return pl.pallas_call(
        add_kernel,
        out_shape=jax.ShapeDtypeStruct(mine.shape, jnp.bfloat16),
        in_specs=[VMEM] * 2,
        out_specs=HBM,
        scratch_shapes=[pltpu.VMEM(mine.shape, jnp.bfloat16), pltpu.SemaphoreType.DMA((GROUPS,))],
        compiler_params=pltpu.CompilerParams(vmem_limit_bytes=8 * 2**20),
    )(own, mine)


def moved(a, axis, by):
    return a if by % 4 == 0 else lax.ppermute(a, axis, [(i, (i + by) % 4) for i in range(4)])


def swap_cores(a):
    return lax.ppermute(a, C, [(0, 1), (1, 0)])


def gradients(queries, grad_out, keys, values, surv_index, counts):
    here = lax.axis_index(X)
    kv, by_depth = pack(keys, values, queries, grad_out, surv_index, counts)
    kv = lax.all_to_all(kv, (X, Z), 0, 0, tiled=True).reshape(16 * TOK, 2 * HEAD_DIM)
    kv_other = swap_cores(kv)
    by_depth = [moved(by_depth[o], "rec", o) for o in range(4)]

    def for_x(p):
        at = lax.rem(here + p, 4)
        return jnp.concatenate([lax.dynamic_slice_in_dim(a, at, 1, axis=0) for a in by_depth], axis=0)

    qg = [moved(for_x(p), X, p) for p in range(4)]
    found = attention_first(qg, kv)
    dq, d_other, products = attention_second(qg, kv, kv_other, found)
    mine = swap_cores(d_other)
    d_own = attention_third(qg, products)
    sums = added(d_own, mine)
    sums = lax.all_to_all(sums.reshape(16, TOK, 2 * HEAD_DIM), (X, Z), 0, 0, tiled=True)
    dq = [moved(dq[o], "rec", -o) for o in range(4)]
    dq = [moved(jnp.stack([dq[o][p] for o in range(4)]), X, -p) for p in range(4)]
    key_grad, value_grad, query_grad = finish(sums, dq)
    return query_grad, key_grad, value_grad


def solution(mesh):
    split = Mesh(mesh.devices.reshape(mesh.shape["rec"], 4, 4, 2), ("rec", X, Z, C))
    return jax.shard_map(
        gradients,
        mesh=split,
        in_specs=(
            P("rec", CTX, None),
            P("rec", CTX, None),
            P(CTX, None),
            P(CTX, None),
            P("rec", None),
            P("rec", None),
        ),
        out_specs=(P("rec", CTX, None), P(CTX, "rec"), P(CTX, "rec")),
        check_vma=False,
    )
```

```python
import math

import jax
import jax.numpy as jnp
from jax import lax
from jax.experimental import pallas as pl
from jax.experimental.pallas import tpu as pltpu
from jax.sharding import Mesh
from jax.sharding import PartitionSpec as P

HEADS = 16
HEAD_DIM = 128
CAP = 32
TOK = 128
X, Z, C = "ctx_0", "ctx_1", "ctx_2"
CTX = (X, Z, C)
GROUPS = 4
CHUNK = 512
QG_ROWS = 72
FACTOR = 1.0 / math.sqrt(HEAD_DIM)
LOG2E = 1.4426950408889634
NEG_FILL = -1e30

NT = (((1,), (1,)), ((), ()))
TN = (((0,), (0,)), ((), ()))
NN = (((1,), (0,)), ((), ()))


def dot(a, b, dims):
    return lax.dot_general(a, b, dims, preferred_element_type=jnp.float32)


def folded(a, op):
    return op(a.reshape(-1, 8, a.shape[1]), axis=0)


def group_operands(qg, x):
    src = lax.rem(lax.axis_index(X) - x + 4, 4)
    q = jnp.concatenate([qg[src, o, 0:CAP, :] for o in range(4)], axis=0)
    g = jnp.concatenate([qg[src, o, CAP : 2 * CAP, :] for o in range(4)], axis=0)
    where = sum(qg[src, o, 2 * CAP : 2 * CAP + 8, :].astype(jnp.float32) for o in range(4))
    place = 8 * x + 2 * lax.axis_index(Z) + lax.axis_index(C)
    return q, g, where[0:1, :].astype(jnp.int32) + place * TOK


def exponentials(kv, part, x, q, g, slot_pos, e_buf, w_buf):
    rows = lax.broadcasted_iota(jnp.int32, (CHUNK, TOK), 0)
    spread = rows + rows // TOK * TOK
    top = jnp.full((8, TOK), NEG_FILL, jnp.float32)
    for k in range(x + 1):
        at = slice(k * CHUNK, (k + 1) * CHUNK)
        score = dot(kv[at, 0:HEAD_DIM], q, NT)
        if k == x:
            score = jnp.where(spread + (2 * k * CHUNK + part * TOK) <= slot_pos, score, NEG_FILL)
        e_buf[at, :] = score
        top = jnp.maximum(top, folded(score, jnp.max))
    top = jnp.max(top, axis=0, keepdims=True)
    total = jnp.zeros((8, TOK), jnp.float32)
    weighted = jnp.zeros((8, TOK), jnp.float32)
    for k in range(x + 1):
        at = slice(k * CHUNK, (k + 1) * CHUNK)
        score = e_buf[at, :]
        e = jnp.exp2((score - top) * (FACTOR * LOG2E))
        if k == x:
            e = jnp.where(score > 0.5 * NEG_FILL, e, 0.0)
        dw = dot(kv[at, HEAD_DIM : 2 * HEAD_DIM], g, NT)
        e_buf[at, :] = e
        w_buf[at, :] = dw
        total = total + folded(e, jnp.sum)
        weighted = weighted + folded(e * dw, jnp.sum)
    return top, jnp.sum(total, axis=0, keepdims=True), jnp.sum(weighted, axis=0, keepdims=True)


def first_kernel(q0, q1, q2, q3, own, e_own, w_own, stats, qg):
    for p, ref in enumerate((q0, q1, q2, q3)):
        qg[p] = ref[...]
    for x in reversed(range(GROUPS)):
        q, g, slot_pos = group_operands(qg, x)
        at = pl.ds(x * (x + 1) // 2 * CHUNK, (x + 1) * CHUNK)
        part = lax.axis_index(C)
        found = exponentials(own, part, x, q, g, slot_pos, e_own.at[at], w_own.at[at])
        for n in range(3):
            stats[8 * x + n : 8 * x + n + 1, :] = found[n]


def second_kernel(*refs):
    q_in, (oth, own, e_own, w_own, stats) = refs[0:4], refs[4:9]
    q_out, (d_oth, ds_own, wb_own) = refs[9:13], refs[13:16]
    qg, dq, e_buf, w_buf, acc = refs[16:]
    for p in range(4):
        qg[p] = q_in[p][...]
    for x in reversed(range(GROUPS)):
        q, g, slot_pos = group_operands(qg, x)
        first = x * (x + 1) // 2 * CHUNK
        top, total, weighted = exponentials(oth, 1 - lax.axis_index(C), x, q, g, slot_pos, e_buf, w_buf)
        own_top, own_total, own_weighted = (stats[8 * x + n : 8 * x + n + 1, :] for n in range(3))
        joint = jnp.maximum(top, own_top)
        oth_scale = jnp.exp2((top - joint) * (FACTOR * LOG2E))
        own_scale = jnp.exp2((own_top - joint) * (FACTOR * LOG2E))
        scale = 1.0 / (total * oth_scale + own_total * own_scale)
        delta = (weighted * oth_scale + own_weighted * own_scale) * scale
        query_sum = jnp.zeros((TOK, HEAD_DIM), jnp.float32)
        for k in range(x + 1):
            rows = slice(k * CHUNK, (k + 1) * CHUNK)
            w = e_buf[rows, :] * (oth_scale * scale)
            ds = (w * (w_buf[rows, :] - delta)).astype(jnp.bfloat16)
            query_sum = query_sum + dot(ds, oth[rows, 0:HEAD_DIM], TN)
            key_part = dot(ds, q, NN)
            value_part = dot(w.astype(jnp.bfloat16), g, NN)
            if x == GROUPS - 1:
                acc[rows, 0:HEAD_DIM] = key_part
                acc[rows, HEAD_DIM : 2 * HEAD_DIM] = value_part
            else:
                acc[rows, 0:HEAD_DIM] += key_part
                acc[rows, HEAD_DIM : 2 * HEAD_DIM] += value_part
        for k in range(x + 1):
            at = slice(first + k * CHUNK, first + (k + 1) * CHUNK)
            w = e_own[at, :] * (own_scale * scale)
            ds = (w * (w_own[at, :] - delta)).astype(jnp.bfloat16)
            query_sum = query_sum + dot(ds, own[k * CHUNK : (k + 1) * CHUNK, 0:HEAD_DIM], TN)
            ds_own[at, :] = ds
            wb_own[at, :] = w.astype(jnp.bfloat16)
        src = lax.rem(lax.axis_index(X) - x + 4, 4)
        query_out = (query_sum * FACTOR).astype(jnp.bfloat16)
        for o in range(4):
            dq[o, src] = query_out[CAP * o : CAP * (o + 1), :]
    for o in range(4):
        q_out[o][...] = dq[o]
    d_oth[:, 0:HEAD_DIM] = (acc[:, 0:HEAD_DIM] * FACTOR).astype(jnp.bfloat16)
    d_oth[:, HEAD_DIM:] = acc[:, HEAD_DIM:].astype(jnp.bfloat16)


def third_kernel(q0, q1, q2, q3, ds_own, wb_own, d_own, qg):
    for p, ref in enumerate((q0, q1, q2, q3)):
        qg[p] = ref[...]
    for x in reversed(range(GROUPS)):
        q, g, _ = group_operands(qg, x)
        for k in range(x + 1):
            rows = slice(k * CHUNK, (k + 1) * CHUNK)
            at = slice(x * (x + 1) // 2 * CHUNK + k * CHUNK, x * (x + 1) // 2 * CHUNK + (k + 1) * CHUNK)
            key_part = dot(ds_own[at, :], q, NN)
            value_part = dot(wb_own[at, :], g, NN)
            if x == GROUPS - 1:
                d_own[rows, 0:HEAD_DIM] = key_part
                d_own[rows, HEAD_DIM : 2 * HEAD_DIM] = value_part
            else:
                d_own[rows, 0:HEAD_DIM] += key_part
                d_own[rows, HEAD_DIM : 2 * HEAD_DIM] += value_part


VMEM = pl.BlockSpec(memory_space=pltpu.VMEM)
HBM = pl.BlockSpec(memory_space=pltpu.HBM)
PAIRS = GROUPS * (GROUPS + 1) // 2 * CHUNK


def kernel_params(mib):
    return pltpu.CompilerParams(vmem_limit_bytes=mib * 2**20)


def attention_first(qg, own):
    return pl.pallas_call(
        first_kernel,
        out_shape=(
            jax.ShapeDtypeStruct((PAIRS, TOK), jnp.float32),
            jax.ShapeDtypeStruct((PAIRS, TOK), jnp.float32),
            jax.ShapeDtypeStruct((8 * GROUPS, TOK), jnp.float32),
        ),
        in_specs=[VMEM] * 5,
        out_specs=(VMEM,) * 3,
        scratch_shapes=[pltpu.VMEM((4, 4, QG_ROWS, HEAD_DIM), jnp.bfloat16)],
        compiler_params=kernel_params(16),
        cost_estimate=pl.CostEstimate(
            flops=2 * 2 * PAIRS * TOK * HEAD_DIM, bytes_accessed=4 * 2**20, transcendentals=PAIRS * TOK
        ),
    )(*qg, own)


def attention_second(qg, own, oth, found):
    keys = own.shape[0]
    out = pl.pallas_call(
        second_kernel,
        out_shape=(jax.ShapeDtypeStruct((4, CAP, HEAD_DIM), jnp.bfloat16),) * 4
        + (
            jax.ShapeDtypeStruct((keys, 2 * HEAD_DIM), jnp.bfloat16),
            jax.ShapeDtypeStruct((PAIRS, TOK), jnp.bfloat16),
            jax.ShapeDtypeStruct((PAIRS, TOK), jnp.bfloat16),
        ),
        in_specs=[VMEM] * 9,
        out_specs=(VMEM,) * 7,
        scratch_shapes=[
            pltpu.VMEM((4, 4, QG_ROWS, HEAD_DIM), jnp.bfloat16),
            pltpu.VMEM((4, 4, CAP, HEAD_DIM), jnp.bfloat16),
            pltpu.VMEM((keys, TOK), jnp.float32),
            pltpu.VMEM((keys, TOK), jnp.float32),
            pltpu.VMEM((keys, 2 * HEAD_DIM), jnp.float32),
        ],
        compiler_params=kernel_params(20),
        cost_estimate=pl.CostEstimate(
            flops=2 * 6 * PAIRS * TOK * HEAD_DIM, bytes_accessed=10 * 2**20, transcendentals=PAIRS * TOK
        ),
    )(*qg, oth, own, *found)
    return out[0:4], out[4], out[5:7]


def attention_third(qg, products):
    return pl.pallas_call(
        third_kernel,
        out_shape=jax.ShapeDtypeStruct((GROUPS * CHUNK, 2 * HEAD_DIM), jnp.float32),
        in_specs=[VMEM] * 6,
        out_specs=VMEM,
        scratch_shapes=[pltpu.VMEM((4, 4, QG_ROWS, HEAD_DIM), jnp.bfloat16)],
        compiler_params=kernel_params(12),
        cost_estimate=pl.CostEstimate(
            flops=2 * 2 * PAIRS * TOK * HEAD_DIM, bytes_accessed=5 * 2**20, transcendentals=0
        ),
    )(*qg, *products)


def pack_kernel(keys, values, queries, grad_out, surv_index, counts, kv, *rest):
    qg, (k_buf, v_buf, kv_buf, q_buf, g_buf, s_buf, c_buf, sems) = rest[0:4], rest[4:]
    depth = lax.axis_index("rec")
    ctx = lax.axis_index(X) * 8 + lax.axis_index(Z) * 2 + lax.axis_index(C)
    half = 2 * HEAD_DIM
    pairs = []
    for h in range(2):
        mine = pl.ds(pl.multiple_of((2 * depth + h) * half, half), half)
        pairs.append((keys.at[:, mine], k_buf.at[:, h * half : (h + 1) * half]))
        pairs.append((values.at[:, mine], v_buf.at[:, h * half : (h + 1) * half]))
    pairs += [(queries.at[0], q_buf), (grad_out.at[0], g_buf), (surv_index, s_buf), (counts, c_buf)]
    copies = [pltpu.make_async_copy(src, dst, sems.at[n]) for n, (src, dst) in enumerate(pairs)]
    for copy in copies:
        copy.start()
    out = []
    for h in range(2):
        copies[2 * h].wait()
        copies[2 * h + 1].wait()
        for x in range(2 * h, 2 * h + 2):
            cols = slice(x * HEAD_DIM, (x + 1) * HEAD_DIM)
            kv_buf[x, :, 0:HEAD_DIM] = k_buf[:, cols]
            kv_buf[x, :, HEAD_DIM:] = v_buf[:, cols]
        part = slice(2 * h, 2 * h + 2)
        for z in range(4):
            out.append(pltpu.make_async_copy(kv_buf.at[part], kv.at[part, z], sems.at[8 + 4 * h + z]))
            out[-1].start()
    for copy in copies[4:]:
        copy.wait()
    live = lax.broadcasted_iota(jnp.int32, (CAP, HEAD_DIM), 0) < c_buf[0, ctx]
    quarter = lax.rem(ctx, 4)
    near = s_buf[0:1, pl.ds(pl.multiple_of(ctx // 4 * TOK, TOK), TOK)]
    lane_group = lax.broadcasted_iota(jnp.int32, (8, TOK), 1) // CAP
    for o in range(4):
        where = pltpu.roll(jnp.broadcast_to(near, (8, TOK)), lax.rem(o - quarter + 4, 4) * CAP, 1)
        where = jnp.where(lane_group == o, where, 0).astype(jnp.float32).astype(jnp.bfloat16)
        for x in range(4):
            head = lax.rem(depth + o, 4) * 4 + x
            cols = pl.ds(pl.multiple_of(head * HEAD_DIM, HEAD_DIM), HEAD_DIM)
            qg[o][x, 0:CAP, :] = q_buf[:, cols]
            grad = jnp.where(live, g_buf[:, cols].astype(jnp.float32), 0.0)
            qg[o][x, CAP : 2 * CAP, :] = grad.astype(jnp.bfloat16)
            qg[o][x, 2 * CAP :, :] = where
    for copy in out:
        copy.wait()


def pack(keys, values, queries, grad_out, surv_index, counts):
    vmem = pl.BlockSpec(memory_space=pltpu.VMEM)
    hbm = pl.BlockSpec(memory_space=pltpu.HBM)
    out = pl.pallas_call(
        pack_kernel,
        out_shape=(jax.ShapeDtypeStruct((4, 4, TOK, 2 * HEAD_DIM), jnp.bfloat16),)
        + (jax.ShapeDtypeStruct((4, QG_ROWS, HEAD_DIM), jnp.bfloat16),) * 4,
        in_specs=[hbm] * 6,
        out_specs=(hbm,) + (vmem,) * 4,
        scratch_shapes=[
            pltpu.VMEM((TOK, 4 * HEAD_DIM), jnp.bfloat16),
            pltpu.VMEM((TOK, 4 * HEAD_DIM), jnp.bfloat16),
            pltpu.VMEM((4, TOK, 2 * HEAD_DIM), jnp.bfloat16),
            pltpu.VMEM((CAP, HEADS * HEAD_DIM), jnp.bfloat16),
            pltpu.VMEM((CAP, HEADS * HEAD_DIM), jnp.bfloat16),
            pltpu.VMEM(surv_index.shape, jnp.int32),
            pltpu.SMEM(counts.shape, jnp.int32),
            pltpu.SemaphoreType.DMA((16,)),
        ],
        compiler_params=pltpu.CompilerParams(vmem_limit_bytes=8 * 2**20),
    )(*(pltpu.with_memory_space_constraint(a, pltpu.HBM) for a in (keys, values, queries, grad_out, surv_index, counts)))
    return out[0].reshape(16, TOK, 2 * HEAD_DIM), out[1:]


def finish_kernel(parts, q0, q1, q2, q3, key_grad, value_grad, query_grad, k_buf, v_buf, q_buf, sems):
    copies = []
    for n, (buf, out, at) in enumerate(((k_buf, key_grad, 0), (v_buf, value_grad, HEAD_DIM))):
        for x in range(4):
            total = sum(parts[4 * x + z, :, at : at + HEAD_DIM].astype(jnp.float32) for z in range(4))
            buf[:, x * HEAD_DIM : (x + 1) * HEAD_DIM] = total.astype(jnp.bfloat16)
        copies.append(pltpu.make_async_copy(buf, out, sems.at[n]))
        copies[n].start()
    depth, here = lax.axis_index("rec"), lax.axis_index(X)
    for p, ref in enumerate((q0, q1, q2, q3)):
        for o in range(4):
            head = lax.rem(depth + o, 4) * 4 + lax.rem(here + p, 4)
            q_buf[:, pl.ds(pl.multiple_of(head * HEAD_DIM, HEAD_DIM), HEAD_DIM)] = ref[o]
    copies.append(pltpu.make_async_copy(q_buf, query_grad.at[0], sems.at[2]))
    copies[2].start()
    for copy in copies:
        copy.wait()


def finish(parts, dq):
    out = jax.ShapeDtypeStruct((TOK, 4 * HEAD_DIM), jnp.bfloat16)
    return pl.pallas_call(
        finish_kernel,
        out_shape=(out, out, jax.ShapeDtypeStruct((1, CAP, HEADS * HEAD_DIM), jnp.bfloat16)),
        in_specs=[VMEM] * 5,
        out_specs=(pl.BlockSpec(memory_space=pl.ANY),) * 3,
        scratch_shapes=[
            pltpu.VMEM((TOK, 4 * HEAD_DIM), jnp.bfloat16),
            pltpu.VMEM((TOK, 4 * HEAD_DIM), jnp.bfloat16),
            pltpu.VMEM((CAP, HEADS * HEAD_DIM), jnp.bfloat16),
            pltpu.SemaphoreType.DMA((3,)),
        ],
        compiler_params=pltpu.CompilerParams(vmem_limit_bytes=8 * 2**20),
    )(parts, *dq)


def add_kernel(own, mine, out, buf, sems):
    copies = []
    for k in range(GROUPS):
        rows = slice(k * CHUNK, (k + 1) * CHUNK)
        other = mine[rows, :].astype(jnp.float32)
        buf[rows, 0:HEAD_DIM] = (own[rows, 0:HEAD_DIM] * FACTOR + other[:, 0:HEAD_DIM]).astype(jnp.bfloat16)
        buf[rows, HEAD_DIM:] = (own[rows, HEAD_DIM:] + other[:, HEAD_DIM:]).astype(jnp.bfloat16)
        copies.append(pltpu.make_async_copy(buf.at[rows], out.at[rows], sems.at[k]))
        copies[k].start()
    for copy in copies:
        copy.wait()


def added(own, mine):
    return pl.pallas_call(
        add_kernel,
        out_shape=jax.ShapeDtypeStruct(mine.shape, jnp.bfloat16),
        in_specs=[VMEM] * 2,
        out_specs=HBM,
        scratch_shapes=[pltpu.VMEM(mine.shape, jnp.bfloat16), pltpu.SemaphoreType.DMA((GROUPS,))],
        compiler_params=pltpu.CompilerParams(vmem_limit_bytes=8 * 2**20),
    )(own, mine)


def moved(a, axis, by):
    return a if by % 4 == 0 else lax.ppermute(a, axis, [(i, (i + by) % 4) for i in range(4)])


def swap_cores(a):
    return lax.ppermute(a, C, [(0, 1), (1, 0)])


def gradients(queries, grad_out, keys, values, surv_index, counts):
    here = lax.axis_index(X)
    kv, by_depth = pack(keys, values, queries, grad_out, surv_index, counts)
    kv = lax.all_to_all(kv, (X, Z), 0, 0, tiled=True).reshape(16 * TOK, 2 * HEAD_DIM)
    kv_other = swap_cores(kv)
    by_depth = [moved(by_depth[o], "rec", o) for o in range(4)]

    def for_x(p):
        at = lax.rem(here + p, 4)
        return jnp.concatenate([lax.dynamic_slice_in_dim(a, at, 1, axis=0) for a in by_depth], axis=0)

    qg = [moved(for_x(p), X, p) for p in range(4)]
    found = attention_first(qg, kv)
    dq, d_other, products = attention_second(qg, kv, kv_other, found)
    mine = swap_cores(d_other)
    d_own = attention_third(qg, products)
    sums = added(d_own, mine)
    sums = lax.all_to_all(sums.reshape(16, TOK, 2 * HEAD_DIM), (X, Z), 0, 0, tiled=True)
    back = []
    for o in range(4):
        back.append(moved(dq[o], "rec", -o))
    dq = []
    for p in range(4):
        dq.append(moved(jnp.stack([back[o][p] for o in range(4)]), X, -p))
    key_grad, value_grad, query_grad = finish(sums, dq)
    return query_grad, key_grad, value_grad


def solution(mesh):
    split = Mesh(mesh.devices.reshape(mesh.shape["rec"], 4, 4, 2), ("rec", X, Z, C))
    return jax.shard_map(
        gradients,
        mesh=split,
        in_specs=(
            P("rec", CTX, None),
            P("rec", CTX, None),
            P(CTX, None),
            P(CTX, None),
            P("rec", None),
            P("rec", None),
        ),
        out_specs=(P("rec", CTX, None), P(CTX, "rec"), P(CTX, "rec")),
        check_vma=False,
    )
```
